32 devices in a mesh: layout: 4 (over z), gx: 4 (over y, core), gy: 2 (over x).
Axes of the slice: x: 2, y: 2, z: 4, core: 2. Of those that a mesh axis runs over, the one named last changes fastest.
Arguments:
- state: float32 [4, 4, 64, 32, 256], P('layout', None, 'gx', None, 'gy'), may hold values from -2 to 2
- planes: float32 [8, 4, 32, 256], P('layout', None, None, 'gy'), may hold values from -2 to 2
- turbine_cell: int32 [4, 64, 32, 256], P('layout', 'gx', None, 'gy'), may hold values from -1 to 15, as said below
- active: int32 [4, 16], P('layout'), may hold values 0 or 1
- yaw_sector: int32 [4, 16], P('layout'), may hold values from 0 to 7
- slot: int32 [4], replicated, may hold values from 0 to 7
Outputs:
- fields: float32 [4, 4, 64, 32, 256], P('layout', None, 'gx', None, 'gy')
The draws below stay inside these ranges and needn't reach their ends.
Inputs may be any that keep to these rules, and one draw needn't show every extreme that they name: `turbine_cell`: cells of value t form turbine t's actuator disk: one streamwise cell, 11 levels around level 16 and 11 spanwise cells (periodic). Every turbine has its disk and disks don't intersect; -1 elsewhere.
All inputs are finite; a program needn't handle non-finite values. No bound on the sum of `active` on one device may be relied on, other than what follows from the above.
Results may differ from the reference program's by a relative error of at most 0.00015.
Values sent between devices are 32-bit elements; how exact they have to be, the bound alone decides.
A program may use at most 64 MiB of HBM per device.

```python
import math
import jax
import jax.numpy as jnp
from jax import lax

NZ = 32
STEPS = 4
SWEEPS = 4
RADIUS = 5
TSPACE = 32
NLAY = 4
NX = 64
NY = 256
TURB = 16
PLANES = 8


def ripple(index, phase):
    return jnp.sin((index + phase).astype(jnp.float32) * (0.5 * math.pi))


def jitter_field(key, extent):
    return jnp.clip(0.3 * jax.random.normal(key, extent, jnp.float32), -0.55, 0.55)


def draw_state(key, part):
    jitter = jitter_field(jax.random.fold_in(key, 101), (NLAY, 4, NX, NZ, NY))
    phases = jax.random.randint(jax.random.fold_in(key, 103), (3, NLAY), 0, 4)
    stream = jnp.arange(NX, dtype=jnp.int32)[None, :, None, None]
    levels = jnp.arange(NZ, dtype=jnp.int32)[None, None, :, None]
    spanwise = jnp.arange(NY, dtype=jnp.int32)[None, None, None, :]
    phase_x = phases[0][:, None, None, None]
    phase_z = phases[1][:, None, None, None]
    phase_y = phases[2][:, None, None, None]
    stream_wind = jitter[:, 0] + 1.4 * ripple(stream, phase_x)
    span_wind = jitter[:, 1] + 1.4 * ripple(spanwise, phase_y)
    vertical_wind = jitter[:, 2] + 0.5 * ripple(levels, phase_z)
    warmth = jitter[:, 3] + 0.6 * ripple(stream + 1, phase_x)
    fields = jnp.stack([stream_wind, span_wind, vertical_wind, warmth], axis=1)
    return jnp.clip(fields, -1.98, 1.98)


def draw_planes(key, part):
    jitter = jitter_field(jax.random.fold_in(key, 201), (PLANES, 4, NZ, NY))
    phases = jax.random.randint(jax.random.fold_in(key, 203), (2, PLANES), 0, 4)
    spanwise = jnp.arange(NY, dtype=jnp.int32)[None, None, :]
    phase_u = phases[0][:, None, None]
    phase_v = phases[1][:, None, None]
    stream_wind = jitter[:, 0] + 0.8 * ripple(spanwise, phase_u)
    span_wind = jitter[:, 1] + 1.4 * ripple(spanwise, phase_v)
    vertical_wind = jitter[:, 2]
    warmth = jitter[:, 3]
    fields = jnp.stack([stream_wind, span_wind, vertical_wind, warmth], axis=1)
    return jnp.clip(fields, -1.98, 1.98)


def draw_turbine_cell(key, part):
    blocks_x = NX // TSPACE
    blocks_y = NY // TSPACE
    key_x = jax.random.fold_in(key, 11)
    key_y = jax.random.fold_in(key, 23)
    offset_x = jax.random.randint(key_x, (NLAY, blocks_x * blocks_y), 0, TSPACE)
    offset_y = jax.random.randint(key_y, (NLAY, blocks_x * blocks_y), RADIUS - TSPACE // 2, TSPACE // 2 - RADIUS)
    stream = jnp.arange(NX)
    span = jnp.arange(NY)
    levels = jnp.arange(NZ)
    block_x = stream // TSPACE
    block_y = (span + TSPACE // 2) // TSPACE % blocks_y
    inside_y = (span + TSPACE // 2) % TSPACE - TSPACE // 2
    turbine = block_x[:, None] * blocks_y + block_y[None, :]
    chosen_x = jnp.take(offset_x, turbine, axis=1)
    chosen_y = jnp.take(offset_y, turbine, axis=1)
    hit = (stream[None, :, None] % TSPACE == chosen_x) & (jnp.abs(inside_y[None, None, :] - chosen_y) <= RADIUS)
    level_hit = jnp.abs(levels - NZ // 2) <= RADIUS
    both = hit[:, :, None, :] & level_hit[None, None, :, None]
    return jnp.where(both, turbine[None, :, None, :], -1).astype(jnp.int32)


def place_ends(values, stream_key, low, largest):
    shape = values.shape
    place = [jax.random.randint(jax.random.fold_in(stream_key, axis), (), 0, shape[axis]) for axis in range(len(shape))]
    values = values.at[tuple(place)].set(low)
    longest = shape.index(max(shape))
    place[longest] = (place[longest] + 1) % shape[longest]
    return values.at[tuple(place)].set(largest)


def setup_inputs(seed: int = 0) -> dict:
    arg_keys = jax.random.split(jax.random.key(seed), 7)
    state = draw_state(jax.random.fold_in(arg_keys[6], 71), 0)
    planes = draw_planes(jax.random.fold_in(arg_keys[6], 71), 0)
    turbine_cell = draw_turbine_cell(jax.random.fold_in(arg_keys[6], 71), 0)
    active = place_ends((jax.random.randint(arg_keys[3], (NLAY, TURB), 0, 4) < 3).astype(jnp.int32), jax.random.fold_in(arg_keys[3], 1), 0, 1)
    yaw_sector = place_ends(jax.random.randint(arg_keys[4], (NLAY, TURB), 0, 8), jax.random.fold_in(arg_keys[4], 1), 0, 7).astype(jnp.int32)
    slot = place_ends(jax.random.randint(arg_keys[5], (STEPS,), 0, PLANES), jax.random.fold_in(arg_keys[5], 1), 0, PLANES - 1).astype(jnp.int32)
    return dict(state=state, planes=planes, turbine_cell=turbine_cell, active=active, yaw_sector=yaw_sector, slot=slot)


TIME_STEP = 0.25
VISCOSITY = 0.02
SMAGORINSKY = 0.0289
DIFFUSIVITY_RATIO = 1.0 / 0.7
BUOYANCY = 0.5
THRUST_COEFF = 1.33
YAW_INCREMENT = 0.1

def profiles(levels):
    height = (jnp.arange(levels).astype(jnp.float32) + 0.5) / levels
    wind_speed = height ** (1.0 / 7.0)
    warmth = 0.5 * height
    zeros = jnp.zeros((levels,), jnp.float32)
    return jnp.stack([wind_speed, zeros, zeros, warmth])

def pad_levels(values):
    keeping = jnp.array([1.0, 1.0, 0.0, 1.0], jnp.float32).reshape(4, 1, 1, 1)
    return jnp.concatenate([values[:, :, :1] * keeping, values, values[:, :, -1:] * keeping], axis=2)

def stencil(padded):
    centre = padded[:, 1:-1, 1:-1, 1:-1]
    along_x = (padded[:, 2:, 1:-1, 1:-1] - padded[:, :-2, 1:-1, 1:-1]) * 0.5
    along_z = (padded[:, 1:-1, 2:, 1:-1] - padded[:, 1:-1, :-2, 1:-1]) * 0.5
    along_y = (padded[:, 1:-1, 1:-1, 2:] - padded[:, 1:-1, 1:-1, :-2]) * 0.5
    laplacian = padded[:, 2:, 1:-1, 1:-1] + padded[:, :-2, 1:-1, 1:-1] + padded[:, 1:-1, 2:, 1:-1] + padded[:, 1:-1, :-2, 1:-1] + padded[:, 1:-1, 1:-1, 2:] + padded[:, 1:-1, 1:-1, :-2] - 6.0 * centre
    return (centre, along_x, along_y, along_z, laplacian)

def tendency(padded, mean_theta, force_u, force_v):
    centre, along_x, along_y, along_z, laplacian = stencil(padded)
    advect = centre[0] * along_x + centre[1] * along_y + centre[2] * along_z
    shear_xy = 0.5 * (along_y[0] + along_x[1])
    shear_xz = 0.5 * (along_z[0] + along_x[2])
    shear_yz = 0.5 * (along_z[1] + along_y[2])
    strain = jnp.sqrt(2.0 * (along_x[0] ** 2 + along_y[1] ** 2 + along_z[2] ** 2) + 4.0 * (shear_xy ** 2 + shear_xz ** 2 + shear_yz ** 2))
    viscous = VISCOSITY + SMAGORINSKY * strain
    scaling = jnp.array([1.0, 1.0, 1.0, DIFFUSIVITY_RATIO], jnp.float32).reshape(4, 1, 1, 1)
    extra = jnp.stack([force_u, force_v, BUOYANCY * (centre[3] - mean_theta[None, :, None]), jnp.zeros_like(force_u)])
    return (centre, laplacian * viscous * scaling - advect + extra)

def disk_terms(values, disk_ids, yaw_angle):
    turbines = yaw_angle.shape[0]
    slot_ids = disk_ids + 1
    cos_cell = jnp.take(jnp.concatenate([jnp.zeros((1,), jnp.float32), jnp.cos(yaw_angle)]), slot_ids)
    sin_cell = jnp.take(jnp.concatenate([jnp.zeros((1,), jnp.float32), jnp.sin(yaw_angle)]), slot_ids)
    normal = values[0] * cos_cell + values[1] * sin_cell
    disk_sums = jax.ops.segment_sum(normal.reshape(-1), slot_ids.reshape(-1), num_segments=turbines + 1)[1:]
    return (cos_cell, sin_cell, disk_sums)

def disk_force(disk_sums, running, disk_ids, cos_cell, sin_cell):
    disk_speed = disk_sums / float((2 * RADIUS + 1) ** 2)
    thrust = -0.5 * THRUST_COEFF * disk_speed * jnp.abs(disk_speed) * running
    per_cell = jnp.take(jnp.concatenate([jnp.zeros((1,), jnp.float32), thrust]), disk_ids + 1)
    return (per_cell * cos_cell, per_cell * sin_cell)

def divergence(extended):
    vertical = extended[2][1:-1, :, 1:-1]
    zeros = jnp.zeros_like(vertical[:, :1])
    padded_w = jnp.concatenate([zeros, vertical, zeros], axis=1)
    return (extended[0][2:, :, 1:-1] - extended[0][:-2, :, 1:-1]) * 0.5 + (extended[1][1:-1, :, 2:] - extended[1][1:-1, :, :-2]) * 0.5 + (padded_w[:, 2:] - padded_w[:, :-2]) * 0.5

def vertical_pair(padded):
    centre = padded[1:-1, :, 1:-1]
    upward = jnp.concatenate([centre[:, 1:], centre[:, -1:]], axis=1)
    downward = jnp.concatenate([centre[:, :1], centre[:, :-1]], axis=1)
    return (upward, downward)

def jacobi(padded, source):
    upward, downward = vertical_pair(padded)
    beside_all = padded[2:, :, 1:-1] + padded[:-2, :, 1:-1] + padded[1:-1, :, 2:] + padded[1:-1, :, :-2] + upward + downward
    return (beside_all - source) / 6.0

def gradient(padded):
    upward, downward = vertical_pair(padded)
    return jnp.stack([(padded[2:, :, 1:-1] - padded[:-2, :, 1:-1]) * 0.5, (padded[1:-1, :, 2:] - padded[1:-1, :, :-2]) * 0.5, (upward - downward) * 0.5])

def wrap_span(values):
    return jnp.concatenate([values[..., -1:], values, values[..., :1]], axis=-1)

def pad_pressure(pressure):
    zeros = jnp.zeros_like(pressure[:1])
    return wrap_span(jnp.concatenate([zeros, pressure, zeros], axis=0))

def advance(fields, inflow, disk_ids, yaw_angle, running):
    theta_sum = lax.optimization_barrier(jnp.sum(fields[3], axis=(0, 2)))
    cos_cell, sin_cell, disk_sums = disk_terms(fields, disk_ids, yaw_angle)
    cell_count = fields.shape[1] * fields.shape[3]
    extended = wrap_span(jnp.concatenate([inflow[:, None], fields, fields[:, -1:]], axis=1))
    force_u, force_v = disk_force(disk_sums, running, disk_ids, cos_cell, sin_cell)
    current, tendencies = tendency(pad_levels(extended), theta_sum / cell_count, force_u, force_v)
    stepped = current + TIME_STEP * tendencies
    provisional = stepped[:3]
    star_ext = wrap_span(jnp.concatenate([inflow[:3, None], provisional, provisional[:, -1:]], axis=1))
    source = divergence(star_ext)
    pressure = -source / 6.0
    for sweep_index in range(SWEEPS):
        pressure = jacobi(pad_pressure(pressure), source)
    gradients = gradient(pad_pressure(pressure))
    return jnp.concatenate([provisional - gradients, stepped[3:]], axis=0)

def reference(state, planes, turbine_cell, active, yaw_sector, slot):
    mean_wind = profiles(state.shape[3])

    def evolve_layout(items):
        start_fields, disk_ids, running, sectors = items
        fields = start_fields + mean_wind[:, None, :, None]
        yaw_angle = (sectors.astype(jnp.float32) - 3.5) * YAW_INCREMENT
        running_f = running.astype(jnp.float32)
        for step_index in range(STEPS):
            inflow = lax.dynamic_index_in_dim(planes, slot[step_index], 0, keepdims=False) + mean_wind[:, :, None]
            fields = advance(fields, inflow, disk_ids, yaw_angle, running_f)
        return fields
    return lax.map(evolve_layout, (state, turbine_cell, active, yaw_sector))
```

```python
import functools

import jax
import jax.numpy as jnp
from jax import lax
from jax.experimental import pallas as pl
from jax.experimental.pallas import tpu as pltpu
from jax.sharding import PartitionSpec as P

STEPS = 4
SWEEPS = 4
RADIUS = 5

TIME_STEP = 0.25
VISCOSITY = 0.02
SMAGORINSKY = 0.0289
DIFFUSIVITY_RATIO = 1.0 / 0.7
BUOYANCY = 0.5
THRUST_COEFF = 1.33
YAW_INCREMENT = 0.1
MESH = pl.DeviceIdType.MESH


def profiles(levels):
    height = (jnp.arange(levels).astype(jnp.float32) + 0.5) / levels
    return jnp.stack([height ** (1.0 / 7.0), 0.5 * height])


def kernel(
    NL, GX, L, R, K, H, turbines, held, columns,
    slot, table, prof, ids, state, planes,
    out,
    F, T, TH, NU, V, W, U, RR, PA, PB, SR, SA, SB, PL, ID, SU, NM, FO, MK, TS, EA, EM, MB, OC, EC, EL, XE,
    i_s, i_r, p_s, p_r, a_s, a_r, b_s, b_r, c_s, c_r, t_s, t_r, loc,
):
    lay = lax.axis_index("layout")
    gx = lax.axis_index("gx")
    gy = lax.axis_index("gy")
    N = GX * L
    s = gx * L + gy
    first = gx == 0
    last = gx == GX - 1
    inner_end = jnp.logical_not(last)
    inner_start = jnp.logical_not(first)
    up_x, down_x = lax.rem(gx + 1, GX), lax.rem(gx + GX - 1, GX)
    up_y, down_y = lax.rem(gy + 1, L), lax.rem(gy + L - 1, L)
    blocks = R // 8
    tiles = blocks + 2
    groups = K // 8
    mid = pl.ds(8, K)
    sides = 1 if L == 2 else 2
    PP = [PA, PB]
    SS = [SA, SB]

    def device_of(t):
        return {"gx": t // L, "gy": lax.rem(t, L)}

    barrier = pltpu.get_barrier_semaphore()
    for d in range(1, N):
        pl.semaphore_signal(barrier, inc=1, device_id=device_of(lax.rem(s + d, N)), device_id_type=MESH)

    @pl.when(first)
    def _():
        for d in range(1, NL):
            pl.semaphore_signal(
                barrier, inc=1, device_id={"layout": lax.rem(lay + d, NL)}, device_id_type=MESH
            )

    own_state = pltpu.make_async_copy(state.at[0, pl.ds(0, 3)], F.at[pl.ds(0, 3), pl.ds(1, R), mid], loc.at[0])
    own_theta = pltpu.make_async_copy(state.at[0, 3], T.at[pl.ds(1, R), mid], loc.at[3])
    own_planes = pltpu.make_async_copy(planes, PL.at[pl.ds(lay * held, held)], loc.at[1])
    own_state.start()
    own_theta.start()

    @pl.when(first)
    def _():
        own_planes.start()

    zero = jnp.zeros((K, 128), jnp.float32)

    @pl.when(first)
    def _():
        for i in range(H):
            RR[i, mid] = zero
        for i in range(sides):
            EL[i, 0] = zero
        XE[0] = zero

    @pl.when(last)
    def _():
        for i in range(H):
            RR[R + H + i, mid] = zero
        for i in range(sides):
            EL[i, tiles - 1] = zero
        XE[1] = zero

    no_level = jnp.zeros((8, 128), jnp.float32)
    for row in range(R):
        W[row, 0:8] = no_level
        W[row, 8 + K:16 + K] = no_level
        F[2, row + 1, 0:8] = no_level
        F[2, row + 1, 8 + K:16 + K] = no_level

    ID[0] = ids[...]

    pl.semaphore_wait(barrier, N - 1 + jnp.where(first, NL - 1, 0))

    class Exchange:
        def __init__(self, send, recv):
            self.send, self.recv, self.items = send, recv, []

        def add(self, tag, src, dst, device, out_if=None, in_if=None):
            i = len(self.items)

            def copy():
                return pltpu.make_async_remote_copy(
                    src_ref=src, dst_ref=dst, send_sem=self.send.at[i], recv_sem=self.recv.at[i],
                    device_id=device, device_id_type=MESH)

            self.items.append((tag, copy, out_if, in_if))
            return self

        def rows(self, tag_up, tag_down, up_src, up_dst, down_src, down_dst):
            self.add(tag_up, up_src, up_dst, {"gx": up_x}, inner_end, inner_start)
            return self.add(tag_down, down_src, down_dst, {"gx": down_x}, inner_start, inner_end)

        def span(self, tag, src, above, below):
            self.add(tag, src, above, {"gy": up_y})
            if sides == 2:
                self.add(tag, src, below, {"gy": down_y})
            return self

        def start(self, *tags):
            for tag, copy, out_if, _ in self.items:
                if tag in tags:
                    if out_if is None:
                        copy().start()
                    else:
                        pl.when(out_if)(lambda: copy().start())

        def wait(self):
            for _, copy, out_if, in_if in self.items:
                if out_if is None:
                    copy().wait()
                else:
                    pl.when(out_if)(lambda: copy().wait_send())
                    pl.when(in_if)(lambda: copy().wait_recv())

    above = sides

    def ids_exchange():
        return Exchange(i_s, i_r).span("s", ID.at[0], ID.at[1], ID.at[above])

    def fields_exchange():
        e = Exchange(a_s, a_r)
        e.rows("r", "r", F.at[:, R, mid], F.at[:, 0, mid], F.at[:, 1, mid], F.at[:, R + 1, mid])
        return e.span("s", EA.at[0], EA.at[1], EA.at[above]).span("s", NM.at[0], NM.at[1], NM.at[above])

    def speed_exchange():
        return Exchange(b_s, b_r).rows("r", "r", U.at[R], U.at[0], U.at[1], U.at[R + 1])

    def source_exchange():
        e = Exchange(c_s, c_r)
        for side, to in ((0, up_y), (1, down_y))[:sides]:
            e.add(blocks - 1, EC.at[blocks - 1], EL.at[side, 0], {"gx": up_x, "gy": to}, inner_end, inner_start)
            e.add(0, EC.at[0], EL.at[side, tiles - 1], {"gx": down_x, "gy": to}, inner_start, inner_end)
        e.rows(
            blocks - 1, 0,
            RR.at[pl.ds(R, H), mid], RR.at[pl.ds(0, H), mid],
            RR.at[pl.ds(H, H), mid], RR.at[pl.ds(H + R, H), mid])
        for b in range(blocks):
            e.span(b, EC.at[b], EL.at[0, b + 1], EL.at[above - 1, b + 1])
        return e.rows(blocks - 1, 0, EC.at[blocks - 1], XE.at[0], EC.at[0], XE.at[1])

    def planes_copy(d):
        return pltpu.make_async_remote_copy(
            src_ref=planes, dst_ref=PL.at[pl.ds(lay * held, held)],
            send_sem=p_s.at[d], recv_sem=p_r.at[d],
            device_id={"layout": lax.rem(lay + d, NL)}, device_id_type=MESH,
        )

    def planes_landing(d):
        source = lax.rem(lay + NL - d, NL)
        return pltpu.make_async_remote_copy(
            src_ref=planes, dst_ref=PL.at[pl.ds(source * held, held)],
            send_sem=p_s.at[d], recv_sem=p_r.at[d],
            device_id={"layout": source}, device_id_type=MESH,
        )

    ids_exchange().start("s")

    @pl.when(first)
    def _():
        for d in range(1, NL):
            planes_copy(d).start()

    lane = lax.broadcasted_iota(jnp.int32, (K, 128), 1)
    level = lax.broadcasted_iota(jnp.int32, (K, 128), 0)
    at_first, at_last = lane == 0, lane == 127
    odd_lane = lax.rem(lane, 2) == 1
    low = K // 2 - RADIUS
    in_band = (level >= low) & (level <= low + 2 * RADIUS)
    lane_8 = lax.broadcasted_iota(jnp.int32, (8, 128), 1)
    level_8 = lax.broadcasted_iota(jnp.int32, (8, 128), 0)
    first_8, last_8 = lane_8 == 0, lane_8 == 127
    place = lax.rem(lane, 16)
    group = lane // 16
    early = place < 8

    def beside_8(f, rim):
        return pltpu.roll(jnp.where(last_8, rim, f), 1, 1), pltpu.roll(jnp.where(first_8, rim, f), 127, 1)

    def put(ref, index, f):
        ref[(*index, mid)] = f
        ref[(*index, pl.ds(7, 1))] = f[0:1]
        ref[(*index, pl.ds(8 + K, 1))] = f[K - 1:K]

    def level_pair(ref, index):
        return ref[(*index, pl.ds(7, K))], ref[(*index, pl.ds(9, K))]

    own_ids = ID[0]
    cosines = jnp.zeros((R, 128), jnp.float32)
    sines, runs = cosines, cosines
    for t in range(turbines):
        here = own_ids == t
        cosines = jnp.where(here, table[0, t], cosines)
        sines = jnp.where(here, table[1, t], sines)
        runs = jnp.where(here, table[2, t], runs)
    FO[2] = cosines
    FO[3] = sines
    FO[4] = runs

    lane_r = lax.broadcasted_iota(jnp.int32, (R, 128), 1)
    shifts = []
    for shift in range(1, 2 * RADIUS + 1):
        shifts.append((1, shift, lane_r >= 128 - shift))
        shifts.append((above, 128 - shift, lane_r < shift))

    def disk_masks():
        names = [ID[0], ID[1], ID[above]]
        for i, (other, amount, wraps) in enumerate(shifts):
            there = names[1] if other == 1 else names[2]
            i_sh = pltpu.roll(jnp.where(wraps, there, names[0]), amount, 1)
            MK[i] = jnp.where(i_sh == names[0], 1.0, 0.0)

    def disk_forces():
        own, before, after = NM[0], NM[1], NM[above]
        total = own
        for i, (other, amount, wraps) in enumerate(shifts):
            n_sh = pltpu.roll(jnp.where(wraps, before if i % 2 == 0 else after, own), amount, 1)
            total = total + jnp.where(MK[i] > 0.5, n_sh, 0.0)
        speed = total / float((2 * RADIUS + 1) ** 2)
        thrust = (-0.5 * THRUST_COEFF * TIME_STEP) * speed * jnp.abs(speed) * FO[4]
        FO[0] = thrust * FO[2]
        FO[1] = thrust * FO[3]

    def disk_sums(row, u, v):
        SU[0, row:row + 1, :] = jnp.sum(jnp.where(in_band, u, 0.0), axis=0, keepdims=True)
        SU[1, row:row + 1, :] = jnp.sum(jnp.where(in_band, v, 0.0), axis=0, keepdims=True)

    def send_span():
        NM[0] = SU[0] * FO[2] + SU[1] * FO[3]
        fields_exchange().start("s")

    width = 128 // groups

    def theta_copy(par, d):
        return pltpu.make_async_remote_copy(
            src_ref=TS.at[par, 0], dst_ref=TS.at[par, d],
            send_sem=t_s.at[par, d], recv_sem=t_r.at[par, d],
            device_id=device_of(lax.rem(s + d, N)), device_id_type=MESH,
        )

    def send_theta(par, total):
        packed = jnp.zeros((8, 128), jnp.float32)
        for g in range(groups):
            part = jnp.sum(total[g * 8:(g + 1) * 8], axis=1, keepdims=True)
            packed = jnp.where(lane_8 // width == g, part, packed)
        TS[par, 0] = packed
        for d in range(1, N):
            theta_copy(par, d).start()

    def mean_theta(par):
        for d in range(1, N):
            theta_copy(par, d).wait()
        total = TS[par, 0]
        for d in range(1, N):
            total = total + TS[par, d]
        total = total * (TIME_STEP * BUOYANCY / columns)
        for g in range(groups):
            MB[8 * g:8 * g + 8] = jnp.broadcast_to(total[:, g * width:g * width + 1], (8, 128))

    def pack2(packed, f, j):
        return jnp.where(lane // 2 == j, pltpu.roll(f, 2 * j + 1, 1), packed)

    def pack16(packed, f, j):
        return jnp.where(group == j, pltpu.roll(f, (16 * j + 8) % 128, 1), packed)

    def unpack16(packed, j):
        return pltpu.roll(packed, (120 - 16 * j) % 128, 1)

    own_theta.wait()
    total = zero
    packed = zero
    for row in range(R):
        warm = T[row + 1, mid] + prof[1]
        put(T, (row + 1,), warm)
        if row in (0, R - 1):
            F[3, row + 1, mid] = warm
        packed = pack2(packed, warm, 3 * R + row)
        total = total + warm
    send_theta(0, total)
    own_state.wait()
    for row in range(R):
        u = F[0, row + 1, mid] + prof[0]
        v = F[1, row + 1, mid]
        put(F, (0, row + 1), u)
        put(F, (1, row + 1), v)
        disk_sums(row, u, v)
        for c, f in enumerate((u, v, F[2, row + 1, mid])):
            packed = pack2(packed, f, c * R + row)
    EA[0] = packed
    fields_exchange().start("r")
    send_span()
    ids_exchange().wait()
    disk_masks()

    @pl.when(first)
    def _():
        own_planes.wait()
        for d in range(1, NL):
            planes_copy(d).wait_send()
            planes_landing(d).wait_recv()

    def rim_of(rims, j):
        return pltpu.roll(rims, 127 - 2 * j, 1)

    def tendency_row(row):
        x = row + 1
        for g in range(groups):
            k = 8 + 8 * g
            rims = EM[8 * g:8 * g + 8]
            cen, dx, dy, dz, around = [], [], [], [], []
            for c in range(3):
                f = F[c, x, k:k + 8]
                xm, xp = F[c, x - 1, k:k + 8], F[c, x + 1, k:k + 8]
                ym, yp = beside_8(f, rim_of(rims, c * R + row))
                km, kp = F[c, x, k - 1:k + 7], F[c, x, k + 1:k + 9]
                cen.append(f)
                dx.append(xp - xm)
                dy.append(yp - ym)
                dz.append(kp - km)
                around.append((xp + xm) + (kp + km) + (yp + ym))
            square = 2.0 * (dx[0] * dx[0] + dy[1] * dy[1] + dz[2] * dz[2])
            for shear in (dy[0] + dx[1], dz[0] + dx[2], dz[1] + dy[2]):
                square = square + shear * shear
            nu = (TIME_STEP * VISCOSITY) + (0.5 * TIME_STEP * SMAGORINSKY) * jnp.sqrt(square)
            NU[row, 8 * g:8 * g + 8] = nu
            remain = 1.0 - 6.0 * nu
            half_u, half_v, half_w = ((0.5 * TIME_STEP) * f for f in cen)
            for c in range(3):
                new = (cen[c] * remain + around[c] * nu) - (half_u * dx[c] + half_v * dy[c] + half_w * dz[c])
                if c < 2:
                    if 8 * g <= low + 2 * RADIUS and 8 * g + 7 >= low:
                        at = level_8 + 8 * g
                        band = (at >= low) & (at <= low + 2 * RADIUS)
                        force = FO[c, pl.ds(row, 1), :]
                        new = new + jnp.where(band, jnp.broadcast_to(force, (8, 128)), 0.0)
                else:
                    new = new + ((TIME_STEP * BUOYANCY) * T[x, k:k + 8] - MB[8 * g:8 * g + 8])
                if c == 0:
                    U[x, 8 * g:8 * g + 8] = new
                elif c == 1:
                    V[row, 8 * g:8 * g + 8] = new
                else:
                    W[row, k:k + 8] = new

    def theta_row(row):
        x = row + 1
        parts = []
        for g in range(groups):
            k = 8 + 8 * g
            f = T[x, k:k + 8]
            xm, xp = T[x - 1, k:k + 8], T[x + 1, k:k + 8]
            ym, yp = beside_8(f, rim_of(EM[8 * g:8 * g + 8], 3 * R + row))
            km, kp = T[x, k - 1:k + 7], T[x, k + 1:k + 9]
            nu = DIFFUSIVITY_RATIO * NU[row, 8 * g:8 * g + 8]
            turn = F[0, x, k:k + 8] * (xp - xm) + F[1, x, k:k + 8] * (yp - ym) + F[2, x, k:k + 8] * (kp - km)
            new = f * (1.0 - 6.0 * nu) + ((xp + xm) + (kp + km) + (yp + ym)) * nu - (0.5 * TIME_STEP) * turn
            TH[row, 8 * g:8 * g + 8] = new
            parts.append(new)
        return parts

    def sources():
        for b in range(blocks):
            packed = zero
            rims = zero
            for j in range(8):
                row = 8 * b + j
                v = V[row]
                v_next = pltpu.roll(v, 1, 1)
                vm = jnp.where(at_first, 0.0, v_next)
                vp = jnp.where(at_last, 0.0, pltpu.roll(v, 127, 1))
                wm, wp = level_pair(W, (row,))
                r = ((U[row + 2] - U[row]) + (vp - vm) + (wp - wm)) * 0.5
                RR[row + H, mid] = r
                packed = pack16(packed, r, j)
                rims = jnp.where(group == j, pltpu.roll(v_next, 16 * j, 1) if j else v_next, rims)
            OC[b] = packed
            EC[b] = jnp.where(place < 2, rims, packed)
            source_exchange().start(b)

    def row_places(t):
        if t == 0:
            return [(i, 8 - H + i) for i in range(H)]
        if t == tiles - 1:
            return [(R + H + i, i) for i in range(H)]
        return [(8 * (t - 1) + j + H, j) for j in range(8)]

    def complete():
        for t in range(tiles):
            if t in (0, tiles - 1):
                clean = zero
                for x, j in row_places(t):
                    clean = pack16(clean, RR[x, mid], j)
                own = XE[0 if t == 0 else 1]
            else:
                clean, own = OC[t - 1], EC[t - 1]
            before, after = EL[0, t], EL[above - 1, t]
            left = jnp.where(early, before, clean)
            left = left + 0.5 * jnp.where(place == 7, pltpu.roll(own, 6, 1), 0.0)
            left = left - 0.5 * jnp.where(place == 8, pltpu.roll(before, 8, 1), 0.0)
            right = jnp.where(early, clean, after)
            right = right + 0.5 * jnp.where(place == 7, pltpu.roll(after, 6, 1), 0.0)
            right = right - 0.5 * jnp.where(place == 8, pltpu.roll(own, 8, 1), 0.0)
            put(SR, (0, t), left)
            put(SR, (1, t), right)
            whole = jnp.where(early, right, left)
            for x, j in row_places(t):
                put(RR, (x,), jnp.where(at_first | at_last, unpack16(whole, j), RR[x, mid]))

    sixth = jnp.float32(1.0 / 6.0)
    at_start = jnp.where(first, 0.0, sixth).astype(jnp.float32)
    at_end = jnp.where(last, 0.0, sixth).astype(jnp.float32)

    def relax(index, around, centre, source, keep):
        if index == 0:
            return (around * (-1.0 / 6.0) - centre) * keep
        return (around - source) * keep

    def sweep(index, v):
        old = RR if index == 0 else PP[(index - 1) % 2]
        new = PP[index % 2]
        for x in range(H - (v - 1), R + H + (v - 1)):
            keep = at_start if x < H else at_end if x >= R + H else sixth
            for g in range(groups):
                k = 8 + 8 * g
                f = old[x, k:k + 8]
                around = (old[x + 1, k:k + 8] + old[x - 1, k:k + 8])
                around = around + (old[x, k - 1:k + 7] + old[x, k + 1:k + 9])
                around = around + (pltpu.roll(f, 1, 1) + pltpu.roll(f, 127, 1))
                p = relax(index, around, f, RR[x, k:k + 8] if index else None, keep)
                new[x, k:k + 8] = p
                if g == 0:
                    new[x, 7:8] = p[0:1]
                if g == groups - 1:
                    new[x, 8 + K:9 + K] = p[7:8]
        old = SR if index == 0 else SS[(index - 1) % 2]
        new = SS[index % 2]
        for side in range(2):
            for t in range(tiles):
                keep = at_start if t == 0 else at_end if t == tiles - 1 else sixth
                f = old[side, t, mid]
                fm = old[side, t - 1, mid] if t else f
                fp = old[side, t + 1, mid] if t < tiles - 1 else f
                km, kp = level_pair(old, (side, t))
                around = pltpu.roll(jnp.where(group == 7, fm, f), 16, 1)
                around = around + pltpu.roll(jnp.where(group == 0, fp, f), 112, 1)
                around = around + (km + kp) + (pltpu.roll(f, 1, 1) + pltpu.roll(f, 127, 1))
                put(new, (side, t), relax(index, around, f, SR[side, t, mid] if index else None, keep))

    def finish(n):
        p, side = PP[(SWEEPS - 1) % 2], SS[(SWEEPS - 1) % 2]
        edge = (lane < SWEEPS) | (lane >= 128 - SWEEPS)
        wholes, rims = [], []
        for t in range(tiles):
            left, right = side[0, t, mid], side[1, t, mid]
            wholes.append(jnp.where(early, right, left))
            rims.append(jnp.where(early, left, right))

        def merge(x, t, j):
            put(p, (x,), jnp.where(edge, unpack16(wholes[t], j), p[x, mid]))

        merge(H - 1, 0, 7)
        merge(R + H, tiles - 1, 0)
        for row in range(R):
            merge(row + H, row // 8 + 1, row % 8)
        packed = zero
        for row in [0, R - 1] + list(range(1, R - 1)):
            x = row + H
            centre = p[x, mid]
            rim = unpack16(rims[row // 8 + 1], row % 8)
            ym = pltpu.roll(jnp.where(at_last, rim, centre), 1, 1)
            yp = pltpu.roll(jnp.where(at_first, rim, centre), 127, 1)
            km, kp = level_pair(p, (x,))
            u = U[row + 1] - 0.5 * (p[x + 1, mid] - p[x - 1, mid])
            v = V[row] - 0.5 * (yp - ym)
            w = W[row, mid] - 0.5 * (kp - km)
            warm = TH[row]
            disk_sums(row, u, v)
            put(F, (0, row + 1), u)
            put(F, (1, row + 1), v)
            F[2, row + 1, mid] = w
            put(T, (row + 1,), warm)
            if row in (0, R - 1):
                F[3, row + 1, mid] = warm
            for c, f in enumerate((u, v, w, warm)):
                packed = pack2(packed, f, c * R + row)
            if row == R - 1:
                pl.when(n < STEPS - 1)(lambda: fields_exchange().start("r"))
        EA[0] = packed

    def step(n, carry):
        par = lax.rem(n, 2)
        fields_exchange().wait()

        @pl.when(first)
        def _():
            plane = slot[n]
            for c in range(4):
                f = PL[plane, c]
                if c in (0, 3):
                    f = f + prof[0 if c == 0 else 1]
                F[c, 0, mid] = f
                if c == 0:
                    U[0] = f

        @pl.when(last)
        def _():
            for c in range(4):
                F[c, R + 1, mid] = F[c, R, mid]

        T[0, mid] = F[3, 0, mid]
        T[R + 1, mid] = F[3, R + 1, mid]
        EM[...] = jnp.where(odd_lane, EA[above], EA[1])
        disk_forces()
        mean_theta(par)

        def pair(i, c):
            tendency_row(i)
            tendency_row(R - 1 - i)
            pl.when(i == 0)(lambda: speed_exchange().start("r"))
            return c

        lax.fori_loop(0, R // 2, pair, 0)

        @pl.when(last)
        def _():
            U[R + 1] = U[R]

        speed_exchange().wait()
        sources()

        def warm_row(row, parts):
            return tuple(a + b for a, b in zip(parts, theta_row(row)))

        parts = lax.fori_loop(0, R, warm_row, tuple(no_level for _ in range(groups)))

        @pl.when(n < STEPS - 1)
        def _():
            send_theta(1 - par, jnp.concatenate(parts, axis=0))

        source_exchange().wait()
        complete()
        for i in range(SWEEPS):
            sweep(i, H - i)
        finish(n)

        @pl.when(n < STEPS - 1)
        def _():
            send_span()

        return carry

    lax.fori_loop(0, STEPS, step, 0)

    own_out = pltpu.make_async_copy(F.at[pl.ds(0, 3), pl.ds(1, R), mid], out.at[0, pl.ds(0, 3)], loc.at[2])
    theta_out = pltpu.make_async_copy(T.at[pl.ds(1, R), mid], out.at[0, 3], loc.at[4])
    own_out.start()
    theta_out.start()
    own_out.wait()
    theta_out.wait()


def solution(mesh):
    NL, GX, L = mesh.shape["layout"], mesh.shape["gx"], mesh.shape["gy"]

    def local(state, planes, turbine_cell, active, yaw_sector, slot):
        rows, K, cols = state.shape[2:]
        R = rows
        H = SWEEPS + 1
        N = GX * L
        turbines = active.shape[1]
        KP, tiles, sides = K + 16, R // 8 + 2, 1 if L == 2 else 2
        held = planes.shape[0]
        ids = turbine_cell[0, :, K // 2, :]
        angle = (yaw_sector[0].astype(jnp.float32) - 3.5) * YAW_INCREMENT
        table = jnp.stack([jnp.cos(angle), jnp.sin(angle), active[0].astype(jnp.float32)])
        prof = jnp.broadcast_to(profiles(K)[:, :, None], (2, K, cols))
        smem = pl.BlockSpec(memory_space=pltpu.SMEM)
        vmem = pl.BlockSpec(memory_space=pltpu.VMEM)
        hbm = pl.BlockSpec(memory_space=pl.ANY)
        f32 = jnp.float32
        dma = pltpu.SemaphoreType.DMA
        return pl.pallas_call(
            functools.partial(
                kernel, NL, GX, L, R, K, H, turbines, held, float(rows * GX * cols * L)
            ),
            out_shape=jax.ShapeDtypeStruct(state.shape, f32),
            in_specs=[smem, smem, vmem, vmem, hbm, hbm],
            out_specs=hbm,
            scratch_shapes=[
                pltpu.VMEM((4, R + 2, KP, cols), f32),
                pltpu.VMEM((R + 2, KP, cols), f32),
                pltpu.VMEM((R, K, cols), f32),
                pltpu.VMEM((R, K, cols), f32),
                pltpu.VMEM((R, K, cols), f32),
                pltpu.VMEM((R, KP, cols), f32),
                pltpu.VMEM((R + 2, K, cols), f32),
                pltpu.VMEM((R + 2 * H, KP, cols), f32),
                pltpu.VMEM((R + 2 * H, KP, cols), f32),
                pltpu.VMEM((R + 2 * H, KP, cols), f32),
                pltpu.VMEM((2, tiles, KP, cols), f32),
                pltpu.VMEM((2, tiles, KP, cols), f32),
                pltpu.VMEM((2, tiles, KP, cols), f32),
                pltpu.VMEM((held * NL, 4, K, cols), f32),
                pltpu.VMEM((sides + 1, R, cols), jnp.int32),
                pltpu.VMEM((2, R, cols), f32),
                pltpu.VMEM((sides + 1, R, cols), f32),
                pltpu.VMEM((5, R, cols), f32),
                pltpu.VMEM((4 * RADIUS, R, cols), f32),
                pltpu.VMEM((2, N, 8, 128), f32),
                pltpu.VMEM((sides + 1, K, cols), f32),
                pltpu.VMEM((K, cols), f32),
                pltpu.VMEM((K, cols), f32),
                pltpu.VMEM((R // 8, K, cols), f32),
                pltpu.VMEM((R // 8, K, cols), f32),
                pltpu.VMEM((sides, tiles, K, cols), f32),
                pltpu.VMEM((2, K, cols), f32),
                dma((2,)), dma((2,)), dma((NL,)), dma((NL,)),
                dma((6,)), dma((6,)), dma((2,)), dma((2,)),
                dma((4 + sides * tiles,)), dma((4 + sides * tiles,)),
                dma((2, N)), dma((2, N)),
                dma((5,)),
            ],
            compiler_params=pltpu.CompilerParams(
                collective_id=0, has_side_effects=True, vmem_limit_bytes=40 * 1024 * 1024
            ),
        )(slot, table, prof, ids, state, planes)

    return jax.shard_map(
        local,
        mesh=mesh,
        in_specs=(
            P("layout", None, "gx", None, "gy"),
            P("layout", None, None, "gy"),
            P("layout", "gx", None, "gy"),
            P("layout", None),
            P("layout", None),
            P(),
        ),
        out_specs=P("layout", None, "gx", None, "gy"),
        check_vma=False,
    )
```

```python
import functools

import jax
import jax.numpy as jnp
from jax import lax
from jax.experimental import pallas as pl
from jax.experimental.pallas import tpu as pltpu
from jax.sharding import PartitionSpec as P

STEPS = 4
SWEEPS = 4
RADIUS = 5

TIME_STEP = 0.25
VISCOSITY = 0.02
SMAGORINSKY = 0.0289
DIFFUSIVITY_RATIO = 1.0 / 0.7
BUOYANCY = 0.5
THRUST_COEFF = 1.33
YAW_INCREMENT = 0.1
MESH = pl.DeviceIdType.MESH


def profiles(levels):
    height = (jnp.arange(levels).astype(jnp.float32) + 0.5) / levels
    return jnp.stack([height ** (1.0 / 7.0), 0.5 * height])


def kernel(
    NL, GX, L, R, K, H, turbines, held, columns,
    slot, table, prof, ids, state, planes,
    out,
    F, T, TH, NU, V, W, U, RR, PA, PB, SR, SA, SB, PL, ID, SU, NM, FO, MK, TS, EA, EM, MB, OC, EC, EL, XE, HP, P0,
    i_s, i_r, p_s, p_r, a_s, a_r, b_s, b_r, c_s, c_r, t_s, t_r, loc,
):
    lay = lax.axis_index("layout")
    gx = lax.axis_index("gx")
    gy = lax.axis_index("gy")
    N = GX * L
    s = gx * L + gy
    first = gx == 0
    last = gx == GX - 1
    inner_end = jnp.logical_not(last)
    inner_start = jnp.logical_not(first)
    up_x, down_x = lax.rem(gx + 1, GX), lax.rem(gx + GX - 1, GX)
    up_y, down_y = lax.rem(gy + 1, L), lax.rem(gy + L - 1, L)
    blocks = R // 8
    tiles = blocks + 2
    groups = K // 8
    mid = pl.ds(8, K)
    sides = 1 if L == 2 else 2
    PP = [PA, PB]
    SS = [SA, SB]

    def device_of(t):
        return {"gx": t // L, "gy": lax.rem(t, L)}

    barrier = pltpu.get_barrier_semaphore()
    for d in range(1, N):
        pl.semaphore_signal(barrier, inc=1, device_id=device_of(lax.rem(s + d, N)), device_id_type=MESH)

    @pl.when(first)
    def _():
        for d in range(1, NL):
            pl.semaphore_signal(
                barrier, inc=1, device_id={"layout": lax.rem(lay + d, NL)}, device_id_type=MESH
            )

    own_state = pltpu.make_async_copy(state.at[0, pl.ds(0, 3)], F.at[pl.ds(0, 3), pl.ds(1, R), mid], loc.at[0])
    own_theta = pltpu.make_async_copy(state.at[0, 3], T.at[pl.ds(1, R), mid], loc.at[3])
    own_planes = pltpu.make_async_copy(planes, PL.at[pl.ds(lay * held, held)], loc.at[1])
    held_planes = pltpu.make_async_copy(planes, HP, loc.at[5])
    own_state.start()
    own_theta.start()

    @pl.when(first)
    def _():
        held_planes.start()
        own_planes.start()

    zero = jnp.zeros((K, 128), jnp.float32)

    @pl.when(first)
    def _():
        for i in range(H):
            RR[i, mid] = zero
        for i in range(sides):
            EL[i, 0] = zero
        XE[0] = zero

    @pl.when(last)
    def _():
        for i in range(H):
            RR[R + H + i, mid] = zero
        for i in range(sides):
            EL[i, tiles - 1] = zero
        XE[1] = zero

    no_level = jnp.zeros((8, 128), jnp.float32)
    for row in range(R):
        W[row, 0:8] = no_level
        W[row, 8 + K:16 + K] = no_level
        F[2, row + 1, 0:8] = no_level
        F[2, row + 1, 8 + K:16 + K] = no_level

    ID[0] = ids[...]

    pl.semaphore_wait(barrier, N - 1 + jnp.where(first, NL - 1, 0))

    class Exchange:
        def __init__(self, send, recv):
            self.send, self.recv, self.items = send, recv, []

        def add(self, tag, src, dst, device, out_if=None, in_if=None):
            i = len(self.items)

            def copy():
                return pltpu.make_async_remote_copy(
                    src_ref=src, dst_ref=dst, send_sem=self.send.at[i], recv_sem=self.recv.at[i],
                    device_id=device, device_id_type=MESH)

            self.items.append((tag, copy, out_if, in_if))
            return self

        def rows(self, tag_up, tag_down, up_src, up_dst, down_src, down_dst):
            self.add(tag_up, up_src, up_dst, {"gx": up_x}, inner_end, inner_start)
            return self.add(tag_down, down_src, down_dst, {"gx": down_x}, inner_start, inner_end)

        def span(self, tag, src, above, below):
            self.add(tag, src, above, {"gy": up_y})
            if sides == 2:
                self.add(tag, src, below, {"gy": down_y})
            return self

        def start(self, *tags):
            for tag, copy, out_if, _ in self.items:
                if tag in tags:
                    if out_if is None:
                        copy().start()
                    else:
                        pl.when(out_if)(lambda: copy().start())

        def wait(self):
            for _, copy, out_if, in_if in self.items:
                if out_if is None:
                    copy().wait()
                else:
                    pl.when(out_if)(lambda: copy().wait_send())
                    pl.when(in_if)(lambda: copy().wait_recv())

    above = sides

    def ids_exchange():
        return Exchange(i_s, i_r).span("s", ID.at[0], ID.at[1], ID.at[above])

    def fields_exchange():
        e = Exchange(a_s, a_r)
        e.rows("r", "r", F.at[:, R, mid], F.at[:, 0, mid], F.at[:, 1, mid], F.at[:, R + 1, mid])
        return e.span("s", EA.at[0], EA.at[1], EA.at[above]).span("s", NM.at[0], NM.at[1], NM.at[above])

    def speed_exchange():
        return Exchange(b_s, b_r).rows("r", "r", U.at[R], U.at[0], U.at[1], U.at[R + 1])

    def source_exchange():
        e = Exchange(c_s, c_r)
        for side, to in ((0, up_y), (1, down_y))[:sides]:
            e.add(blocks - 1, EC.at[blocks - 1], EL.at[side, 0], {"gx": up_x, "gy": to}, inner_end, inner_start)
            e.add(0, EC.at[0], EL.at[side, tiles - 1], {"gx": down_x, "gy": to}, inner_start, inner_end)
        e.rows(
            blocks - 1, 0,
            RR.at[pl.ds(R, H), mid], RR.at[pl.ds(0, H), mid],
            RR.at[pl.ds(H, H), mid], RR.at[pl.ds(H + R, H), mid])
        for b in range(blocks):
            e.span(b, EC.at[b], EL.at[0, b + 1], EL.at[above - 1, b + 1])
        return e.rows(blocks - 1, 0, EC.at[blocks - 1], XE.at[0], EC.at[0], XE.at[1])

    def planes_copy(d):
        return pltpu.make_async_remote_copy(
            src_ref=planes, dst_ref=PL.at[pl.ds(lay * held, held)],
            send_sem=p_s.at[d], recv_sem=p_r.at[d],
            device_id={"layout": lax.rem(lay + d, NL)}, device_id_type=MESH,
        )

    def planes_landing(d):
        source = lax.rem(lay + NL - d, NL)
        return pltpu.make_async_remote_copy(
            src_ref=planes, dst_ref=PL.at[pl.ds(source * held, held)],
            send_sem=p_s.at[d], recv_sem=p_r.at[d],
            device_id={"layout": source}, device_id_type=MESH,
        )

    def first_plane(d, source):
        return pltpu.make_async_remote_copy(
            src_ref=P0.at[lay], dst_ref=P0.at[source],
            send_sem=p_s.at[NL + d], recv_sem=p_r.at[NL + d],
            device_id={"layout": lax.rem(lay + d, NL)}, device_id_type=MESH,
        )

    ids_exchange().start("s")

    @pl.when(first)
    def _():
        held_planes.wait()
        near = jnp.minimum(jnp.maximum(slot[0] - lay * held, 0), held - 1)
        for c in range(4):
            P0[lay, c] = HP[near, c]
        for d in range(1, NL):
            first_plane(d, lay).start()
        for d in range(1, NL):
            planes_copy(d).start()

    lane = lax.broadcasted_iota(jnp.int32, (K, 128), 1)
    level = lax.broadcasted_iota(jnp.int32, (K, 128), 0)
    at_first, at_last = lane == 0, lane == 127
    odd_lane = lax.rem(lane, 2) == 1
    low = K // 2 - RADIUS
    in_band = (level >= low) & (level <= low + 2 * RADIUS)
    lane_8 = lax.broadcasted_iota(jnp.int32, (8, 128), 1)
    level_8 = lax.broadcasted_iota(jnp.int32, (8, 128), 0)
    around_end = lax.rem(lane + 1, 128)
    window = lax.rem(lane + 8, 128)
    place = lax.rem(window, 16)
    group = window // 16
    early = place < 8

    def beside(f, rim):
        return pltpu.roll(jnp.where(at_last, rim, f), 1, 1), pltpu.roll(jnp.where(at_first, rim, f), 127, 1)

    def put(ref, index, f):
        ref[(*index, mid)] = f
        ref[(*index, pl.ds(7, 1))] = f[0:1]
        ref[(*index, pl.ds(8 + K, 1))] = f[K - 1:K]

    def level_pair(ref, index):
        return ref[(*index, pl.ds(7, K))], ref[(*index, pl.ds(9, K))]

    own_ids = ID[0]
    cosines = jnp.zeros((R, 128), jnp.float32)
    sines, runs = cosines, cosines
    for t in range(turbines):
        here = own_ids == t
        cosines = jnp.where(here, table[0, t], cosines)
        sines = jnp.where(here, table[1, t], sines)
        runs = jnp.where(here, table[2, t], runs)
    FO[2] = cosines
    FO[3] = sines
    FO[4] = runs

    lane_r = lax.broadcasted_iota(jnp.int32, (R, 128), 1)
    shifts = []
    for shift in range(1, 2 * RADIUS + 1):
        shifts.append((1, shift, lane_r >= 128 - shift))
        shifts.append((above, 128 - shift, lane_r < shift))

    def disk_masks():
        names = [ID[0], ID[1], ID[above]]
        for i, (other, amount, wraps) in enumerate(shifts):
            there = names[1] if other == 1 else names[2]
            i_sh = pltpu.roll(jnp.where(wraps, there, names[0]), amount, 1)
            MK[i] = jnp.where(i_sh == names[0], 1.0, 0.0)

    def disk_forces():
        own, before, after = NM[0], NM[1], NM[above]
        total = own
        for i, (other, amount, wraps) in enumerate(shifts):
            n_sh = pltpu.roll(jnp.where(wraps, before if i % 2 == 0 else after, own), amount, 1)
            total = total + jnp.where(MK[i] > 0.5, n_sh, 0.0)
        speed = total / float((2 * RADIUS + 1) ** 2)
        thrust = (-0.5 * THRUST_COEFF * TIME_STEP) * speed * jnp.abs(speed) * FO[4]
        FO[0] = thrust * FO[2]
        FO[1] = thrust * FO[3]

    def disk_sums(row, u, v):
        SU[0, row:row + 1, :] = jnp.sum(jnp.where(in_band, u, 0.0), axis=0, keepdims=True)
        SU[1, row:row + 1, :] = jnp.sum(jnp.where(in_band, v, 0.0), axis=0, keepdims=True)

    def send_span():
        NM[0] = SU[0] * FO[2] + SU[1] * FO[3]
        fields_exchange().start("s")

    width = 128 // groups

    def theta_copy(par, d):
        return pltpu.make_async_remote_copy(
            src_ref=TS.at[par, 0], dst_ref=TS.at[par, d],
            send_sem=t_s.at[par, d], recv_sem=t_r.at[par, d],
            device_id=device_of(lax.rem(s + d, N)), device_id_type=MESH,
        )

    def send_theta(par, total):
        packed = jnp.zeros((8, 128), jnp.float32)
        for g in range(groups):
            part = jnp.sum(total[g * 8:(g + 1) * 8], axis=1, keepdims=True)
            packed = jnp.where(lane_8 // width == g, part, packed)
        TS[par, 0] = packed
        for d in range(1, N):
            theta_copy(par, d).start()

    def mean_theta(par):
        for d in range(1, N):
            theta_copy(par, d).wait()
        total = TS[par, 0]
        for d in range(1, N):
            total = total + TS[par, d]
        total = total * (TIME_STEP * BUOYANCY / columns)
        for g in range(groups):
            MB[8 * g:8 * g + 8] = jnp.broadcast_to(total[:, g * width:g * width + 1], (8, 128))

    def gather(items, place_of, width):
        while len(items) > 1:
            merged = []
            for a, b in zip(items[::2], items[1::2]):
                if a is None and b is None:
                    merged.append(None)
                    continue
                moved = zero if b is None else pltpu.roll(b, width, 1)
                merged.append(jnp.where(place_of < width, zero if a is None else a, moved))
            items, width = merged, 2 * width
        return items[0]

    def unpack16(packed, j):
        return pltpu.roll(packed, 128 - 16 * j, 1) if j else packed

    own_theta.wait()
    total = zero
    for row in range(R):
        warm = T[row + 1, mid] + prof[1]
        put(T, (row + 1,), warm)
        if row in (0, R - 1):
            F[3, row + 1, mid] = warm
        total = total + warm
    send_theta(0, total)
    own_state.wait()
    rims = []
    for row in range(R):
        u = F[0, row + 1, mid] + prof[0]
        v = F[1, row + 1, mid]
        put(F, (0, row + 1), u)
        put(F, (1, row + 1), v)
        disk_sums(row, u, v)
        rims.append(gather([u, v, F[2, row + 1, mid], T[row + 1, mid]], around_end, 2))
    EA[0] = gather(rims, around_end, 8)
    fields_exchange().start("r")
    send_span()
    ids_exchange().wait()
    disk_masks()

    def rim_of(row, c):
        return pltpu.roll(EM[...], lax.rem(128 - 8 * row - 2 * c, 128), 1)

    def tendency_row(row):
        x = row + 1
        y_pairs = [beside(F[c, x, mid], rim_of(row, c)) for c in range(3)]
        for g in range(groups):
            k = 8 + 8 * g
            cen, dx, dy, dz, around = [], [], [], [], []
            for c in range(3):
                f = F[c, x, k:k + 8]
                xm, xp = F[c, x - 1, k:k + 8], F[c, x + 1, k:k + 8]
                ym, yp = (f_y[8 * g:8 * g + 8] for f_y in y_pairs[c])
                km, kp = F[c, x, k - 1:k + 7], F[c, x, k + 1:k + 9]
                cen.append(f)
                dx.append(xp - xm)
                dy.append(yp - ym)
                dz.append(kp - km)
                around.append((xp + xm) + (kp + km) + (yp + ym))
            square = 2.0 * (dx[0] * dx[0] + dy[1] * dy[1] + dz[2] * dz[2])
            for shear in (dy[0] + dx[1], dz[0] + dx[2], dz[1] + dy[2]):
                square = square + shear * shear
            nu = (TIME_STEP * VISCOSITY) + (0.5 * TIME_STEP * SMAGORINSKY) * jnp.sqrt(square)
            NU[row, 8 * g:8 * g + 8] = nu
            remain = 1.0 - 6.0 * nu
            half_u, half_v, half_w = ((0.5 * TIME_STEP) * f for f in cen)
            for c in range(3):
                new = (cen[c] * remain + around[c] * nu) - (half_u * dx[c] + half_v * dy[c] + half_w * dz[c])
                if c < 2:
                    if 8 * g <= low + 2 * RADIUS and 8 * g + 7 >= low:
                        at = level_8 + 8 * g
                        band = (at >= low) & (at <= low + 2 * RADIUS)
                        force = FO[c, pl.ds(row, 1), :]
                        new = new + jnp.where(band, jnp.broadcast_to(force, (8, 128)), 0.0)
                else:
                    new = new + ((TIME_STEP * BUOYANCY) * T[x, k:k + 8] - MB[8 * g:8 * g + 8])
                if c == 0:
                    U[x, 8 * g:8 * g + 8] = new
                elif c == 1:
                    V[row, 8 * g:8 * g + 8] = new
                else:
                    W[row, k:k + 8] = new

    def theta_row(row):
        x = row + 1
        y_pair = beside(T[x, mid], rim_of(row, 3))
        parts = []
        for g in range(groups):
            k = 8 + 8 * g
            f = T[x, k:k + 8]
            xm, xp = T[x - 1, k:k + 8], T[x + 1, k:k + 8]
            ym, yp = (f_y[8 * g:8 * g + 8] for f_y in y_pair)
            km, kp = T[x, k - 1:k + 7], T[x, k + 1:k + 9]
            nu = DIFFUSIVITY_RATIO * NU[row, 8 * g:8 * g + 8]
            turn = F[0, x, k:k + 8] * (xp - xm) + F[1, x, k:k + 8] * (yp - ym) + F[2, x, k:k + 8] * (kp - km)
            new = f * (1.0 - 6.0 * nu) + ((xp + xm) + (kp + km) + (yp + ym)) * nu - (0.5 * TIME_STEP) * turn
            TH[row, 8 * g:8 * g + 8] = new
            parts.append(new)
        return parts

    def sources():
        for b in range(blocks):
            rows, rims = [], []
            for j in range(8):
                row = 8 * b + j
                v = V[row]
                v_next = pltpu.roll(v, 1, 1)
                vm = jnp.where(at_first, 0.0, v_next)
                vp = jnp.where(at_last, 0.0, pltpu.roll(v, 127, 1))
                wm, wp = level_pair(W, (row,))
                r = ((U[row + 2] - U[row]) + (vp - vm) + (wp - wm)) * 0.5
                RR[row + H, mid] = r
                rows.append(r)
                rims.append(v_next)
            packed = gather(rows, window, 16)
            OC[b] = packed
            EC[b] = jnp.where(place < 2, pltpu.roll(gather(rims, lane, 16), 120, 1), packed)
            source_exchange().start(b)

    def row_places(t):
        if t == 0:
            return [(i, 8 - H + i) for i in range(H)]
        if t == tiles - 1:
            return [(R + H + i, i) for i in range(H)]
        return [(8 * (t - 1) + j + H, j) for j in range(8)]

    def complete():
        wholes = []
        for t in range(tiles):
            if t in (0, tiles - 1):
                known = dict((j, x) for x, j in row_places(t))
                clean = gather([RR[known[j], mid] if j in known else None for j in range(8)], window, 16)
                own = XE[0 if t == 0 else 1]
            else:
                clean, own = OC[t - 1], EC[t - 1]
            before, after = EL[0, t], EL[above - 1, t]
            left = jnp.where(early, before, clean)
            left = left + 0.5 * jnp.where(place == 7, pltpu.roll(own, 6, 1), 0.0)
            left = left - 0.5 * jnp.where(place == 8, pltpu.roll(before, 8, 1), 0.0)
            right = jnp.where(early, clean, after)
            right = right + 0.5 * jnp.where(place == 7, pltpu.roll(after, 6, 1), 0.0)
            right = right - 0.5 * jnp.where(place == 8, pltpu.roll(own, 8, 1), 0.0)
            put(SR, (0, t), left)
            put(SR, (1, t), right)
            wholes.append(jnp.where(early, right, left))
        for slot_j in range(8):
            for t in range(tiles):
                for x, j in row_places(t):
                    if j == slot_j:
                        put(RR, (x,), jnp.where(at_first | at_last, unpack16(wholes[t], j), RR[x, mid]))

    sixth = jnp.float32(1.0 / 6.0)
    at_start = jnp.where(first, 0.0, sixth).astype(jnp.float32)
    at_end = jnp.where(last, 0.0, sixth).astype(jnp.float32)

    def relax(index, around, centre, source, keep):
        if index == 0:
            return (around * (-1.0 / 6.0) - centre) * keep
        return (around - source) * keep

    def sweep(index, v):
        old = RR if index == 0 else PP[(index - 1) % 2]
        new = PP[index % 2]
        for x in range(H - (v - 1), R + H + (v - 1)):
            keep = at_start if x < H else at_end if x >= R + H else sixth
            for g in range(groups):
                k = 8 + 8 * g
                f = old[x, k:k + 8]
                around = (old[x + 1, k:k + 8] + old[x - 1, k:k + 8])
                around = around + (old[x, k - 1:k + 7] + old[x, k + 1:k + 9])
                around = around + (pltpu.roll(f, 1, 1) + pltpu.roll(f, 127, 1))
                p = relax(index, around, f, RR[x, k:k + 8] if index else None, keep)
                new[x, k:k + 8] = p
                if g == 0:
                    new[x, 7:8] = p[0:1]
                if g == groups - 1:
                    new[x, 8 + K:9 + K] = p[7:8]
        old = SR if index == 0 else SS[(index - 1) % 2]
        new = SS[index % 2]
        for side in range(2):
            for t in range(tiles):
                keep = at_start if t == 0 else at_end if t == tiles - 1 else sixth
                f = old[side, t, mid]
                fm = old[side, t - 1, mid] if t else f
                fp = old[side, t + 1, mid] if t < tiles - 1 else f
                km, kp = level_pair(old, (side, t))
                around = pltpu.roll(jnp.where(group == 7, fm, f), 16, 1)
                around = around + pltpu.roll(jnp.where(group == 0, fp, f), 112, 1)
                around = around + (km + kp) + (pltpu.roll(f, 1, 1) + pltpu.roll(f, 127, 1))
                put(new, (side, t), relax(index, around, f, SR[side, t, mid] if index else None, keep))

    def finish(n):
        p, side = PP[(SWEEPS - 1) % 2], SS[(SWEEPS - 1) % 2]
        edge = (lane < SWEEPS) | (lane >= 128 - SWEEPS)
        wholes, rims = [], []
        for t in range(tiles):
            left, right = side[0, t, mid], side[1, t, mid]
            wholes.append(jnp.where(early, right, left))
            rims.append(jnp.where(early, left, right))

        def merge(x, t, j):
            put(p, (x,), jnp.where(edge, unpack16(wholes[t], j), p[x, mid]))

        merge(H - 1, 0, 7)
        merge(R + H, tiles - 1, 0)
        for j in range(8):
            for b in range(blocks):
                merge(8 * b + j + H, b + 1, j)
                RR[8 * b + j + H, mid] = unpack16(rims[b + 1], j)
        rows = [None] * R
        for row in [0, R - 1] + list(range(1, R - 1)):
            x = row + H
            centre = p[x, mid]
            rim = RR[x, mid]
            ym = pltpu.roll(jnp.where(at_last, rim, centre), 1, 1)
            yp = pltpu.roll(jnp.where(at_first, rim, centre), 127, 1)
            km, kp = level_pair(p, (x,))
            u = U[row + 1] - 0.5 * (p[x + 1, mid] - p[x - 1, mid])
            v = V[row] - 0.5 * (yp - ym)
            w = W[row, mid] - 0.5 * (kp - km)
            warm = TH[row]
            disk_sums(row, u, v)
            put(F, (0, row + 1), u)
            put(F, (1, row + 1), v)
            F[2, row + 1, mid] = w
            put(T, (row + 1,), warm)
            if row in (0, R - 1):
                F[3, row + 1, mid] = warm
            rows[row] = gather([u, v, w, warm], around_end, 2)
            if row == R - 1:
                pl.when(n < STEPS - 1)(lambda: fields_exchange().start("r"))
        EA[0] = gather(rows, around_end, 8)

    def step(n, carry):
        par = lax.rem(n, 2)
        fields_exchange().wait()

        def inflow(held_in, index):
            for c in range(4):
                f = held_in[index, c]
                if c in (0, 3):
                    f = f + prof[0 if c == 0 else 1]
                F[c, 0, mid] = f
                if c == 0:
                    U[0] = f

        @pl.when(first & (n == 0))
        def _():
            for d in range(1, NL):
                first_plane(d, lay).wait_send()
                first_plane(d, lax.rem(lay + NL - d, NL)).wait_recv()
            inflow(P0, lax.div(slot[0], held))

        @pl.when(first & (n == 1))
        def _():
            own_planes.wait()
            for d in range(1, NL):
                planes_copy(d).wait_send()
                planes_landing(d).wait_recv()

        @pl.when(first & (n > 0))
        def _():
            inflow(PL, slot[n])

        @pl.when(last)
        def _():
            for c in range(4):
                F[c, R + 1, mid] = F[c, R, mid]

        T[0, mid] = F[3, 0, mid]
        T[R + 1, mid] = F[3, R + 1, mid]
        EM[...] = jnp.where(odd_lane, EA[1], EA[above])
        disk_forces()
        mean_theta(par)

        def pair(i, c):
            tendency_row(i)
            tendency_row(R - 1 - i)
            pl.when(i == 0)(lambda: speed_exchange().start("r"))
            return c

        lax.fori_loop(0, R // 2, pair, 0)

        @pl.when(last)
        def _():
            U[R + 1] = U[R]

        speed_exchange().wait()
        sources()

        def warm_row(row, parts):
            return tuple(a + b for a, b in zip(parts, theta_row(row)))

        parts = lax.fori_loop(
            0, R // 2, lambda i, c: warm_row(2 * i + 1, warm_row(2 * i, c)), tuple(no_level for _ in range(groups)))

        @pl.when(n < STEPS - 1)
        def _():
            send_theta(1 - par, jnp.concatenate(parts, axis=0))

        source_exchange().wait()
        complete()
        for i in range(SWEEPS):
            sweep(i, H - i)
        finish(n)

        @pl.when(n < STEPS - 1)
        def _():
            send_span()

        return carry

    lax.fori_loop(0, STEPS, step, 0)

    own_out = pltpu.make_async_copy(F.at[pl.ds(0, 3), pl.ds(1, R), mid], out.at[0, pl.ds(0, 3)], loc.at[2])
    theta_out = pltpu.make_async_copy(T.at[pl.ds(1, R), mid], out.at[0, 3], loc.at[4])
    own_out.start()
    theta_out.start()
    own_out.wait()
    theta_out.wait()


def solution(mesh):
    NL, GX, L = mesh.shape["layout"], mesh.shape["gx"], mesh.shape["gy"]

    def local(state, planes, turbine_cell, active, yaw_sector, slot):
        rows, K, cols = state.shape[2:]
        R = rows
        H = SWEEPS + 1
        N = GX * L
        turbines = active.shape[1]
        KP, tiles, sides = K + 16, R // 8 + 2, 1 if L == 2 else 2
        held = planes.shape[0]
        ids = turbine_cell[0, :, K // 2, :]
        angle = (yaw_sector[0].astype(jnp.float32) - 3.5) * YAW_INCREMENT
        table = jnp.stack([jnp.cos(angle), jnp.sin(angle), active[0].astype(jnp.float32)])
        prof = jnp.broadcast_to(profiles(K)[:, :, None], (2, K, cols))
        smem = pl.BlockSpec(memory_space=pltpu.SMEM)
        vmem = pl.BlockSpec(memory_space=pltpu.VMEM)
        hbm = pl.BlockSpec(memory_space=pl.ANY)
        f32 = jnp.float32
        dma = pltpu.SemaphoreType.DMA
        return pl.pallas_call(
            functools.partial(
                kernel, NL, GX, L, R, K, H, turbines, held, float(rows * GX * cols * L)
            ),
            out_shape=jax.ShapeDtypeStruct(state.shape, f32),
            in_specs=[smem, smem, vmem, vmem, hbm, hbm],
            out_specs=hbm,
            scratch_shapes=[
                pltpu.VMEM((4, R + 2, KP, cols), f32),
                pltpu.VMEM((R + 2, KP, cols), f32),
                pltpu.VMEM((R, K, cols), f32),
                pltpu.VMEM((R, K, cols), f32),
                pltpu.VMEM((R, K, cols), f32),
                pltpu.VMEM((R, KP, cols), f32),
                pltpu.VMEM((R + 2, K, cols), f32),
                pltpu.VMEM((R + 2 * H, KP, cols), f32),
                pltpu.VMEM((R + 2 * H, KP, cols), f32),
                pltpu.VMEM((R + 2 * H, KP, cols), f32),
                pltpu.VMEM((2, tiles, KP, cols), f32),
                pltpu.VMEM((2, tiles, KP, cols), f32),
                pltpu.VMEM((2, tiles, KP, cols), f32),
                pltpu.VMEM((held * NL, 4, K, cols), f32),
                pltpu.VMEM((sides + 1, R, cols), jnp.int32),
                pltpu.VMEM((2, R, cols), f32),
                pltpu.VMEM((sides + 1, R, cols), f32),
                pltpu.VMEM((5, R, cols), f32),
                pltpu.VMEM((4 * RADIUS, R, cols), f32),
                pltpu.VMEM((2, N, 8, 128), f32),
                pltpu.VMEM((sides + 1, K, cols), f32),
                pltpu.VMEM((K, cols), f32),
                pltpu.VMEM((K, cols), f32),
                pltpu.VMEM((R // 8, K, cols), f32),
                pltpu.VMEM((R // 8, K, cols), f32),
                pltpu.VMEM((sides, tiles, K, cols), f32),
                pltpu.VMEM((2, K, cols), f32),
                pltpu.VMEM((held, 4, K, cols), f32),
                pltpu.VMEM((NL, 4, K, cols), f32),
                dma((2,)), dma((2,)), dma((2 * NL,)), dma((2 * NL,)),
                dma((6,)), dma((6,)), dma((2,)), dma((2,)),
                dma((4 + sides * tiles,)), dma((4 + sides * tiles,)),
                dma((2, N)), dma((2, N)),
                dma((6,)),
            ],
            compiler_params=pltpu.CompilerParams(
                collective_id=0, has_side_effects=True, vmem_limit_bytes=60 * 1024 * 1024
            ),
        )(slot, table, prof, ids, state, planes)

    return jax.shard_map(
        local,
        mesh=mesh,
        in_specs=(
            P("layout", None, "gx", None, "gy"),
            P("layout", None, None, "gy"),
            P("layout", "gx", None, "gy"),
            P("layout", None),
            P("layout", None),
            P(),
        ),
        out_specs=P("layout", None, "gx", None, "gy"),
        check_vma=False,
    )
```

```python
import functools

import jax
import jax.numpy as jnp
from jax import lax
from jax.experimental import pallas as pl
from jax.experimental.pallas import tpu as pltpu
from jax.sharding import PartitionSpec as P

STEPS = 4
SWEEPS = 4
RADIUS = 5

TIME_STEP = 0.25
VISCOSITY = 0.02
SMAGORINSKY = 0.0289
DIFFUSIVITY_RATIO = 1.0 / 0.7
BUOYANCY = 0.5
THRUST_COEFF = 1.33
YAW_INCREMENT = 0.1
MESH = pl.DeviceIdType.MESH


def kernel(
    NL, GX, L, R, K, H, turbines, held, columns,
    slot, active, yaw_sector, cells, state, planes,
    out,
    F, T, TH, NU, V, W, U, RR, PA, PB, SR, SA, SB, PL, ID, SU, NM, FO, MK, TS, EA, EM, MB, OC, EC, EL, XE, HP, P0, prof,
    i_s, i_r, p_s, p_r, a_s, a_r, b_s, b_r, c_s, c_r, t_s, t_r, loc,
):
    lay = lax.axis_index("layout")
    gx = lax.axis_index("gx")
    gy = lax.axis_index("gy")
    N = GX * L
    s = gx * L + gy
    first = gx == 0
    last = gx == GX - 1
    inner_end = jnp.logical_not(last)
    inner_start = jnp.logical_not(first)
    up_x, down_x = lax.rem(gx + 1, GX), lax.rem(gx + GX - 1, GX)
    up_y, down_y = lax.rem(gy + 1, L), lax.rem(gy + L - 1, L)
    blocks = R // 8
    tiles = blocks + 2
    groups = K // 8
    mid = pl.ds(8, K)
    sides = 1 if L == 2 else 2
    PP = [PA, PB]
    SS = [SA, SB]

    def device_of(t):
        return {"gx": t // L, "gy": lax.rem(t, L)}

    barrier = pltpu.get_barrier_semaphore()
    for d in range(1, N):
        pl.semaphore_signal(barrier, inc=1, device_id=device_of(lax.rem(s + d, N)), device_id_type=MESH)

    @pl.when(first)
    def _():
        for d in range(1, NL):
            pl.semaphore_signal(
                barrier, inc=1, device_id={"layout": lax.rem(lay + d, NL)}, device_id_type=MESH
            )

    own_state = pltpu.make_async_copy(state.at[0, pl.ds(0, 3)], F.at[pl.ds(0, 3), pl.ds(1, R), mid], loc.at[0])
    own_theta = pltpu.make_async_copy(state.at[0, 3], T.at[pl.ds(1, R), mid], loc.at[3])
    own_planes = pltpu.make_async_copy(planes, PL.at[pl.ds(lay * held, held)], loc.at[1])
    held_planes = pltpu.make_async_copy(planes, HP, loc.at[5])
    own_ids_copy = pltpu.make_async_copy(cells.at[0, :, K // 2], ID.at[0], loc.at[6])
    own_ids_copy.start()
    own_theta.start()
    own_state.start()

    @pl.when(first)
    def _():
        held_planes.start()
        own_planes.start()

    zero = jnp.zeros((K, 128), jnp.float32)

    @pl.when(first)
    def _():
        for i in range(H):
            RR[i, mid] = zero
        for i in range(sides):
            EL[i, 0] = zero
        XE[0] = zero

    @pl.when(last)
    def _():
        for i in range(H):
            RR[R + H + i, mid] = zero
        for i in range(sides):
            EL[i, tiles - 1] = zero
        XE[1] = zero

    height = (lax.broadcasted_iota(jnp.int32, (K, 128), 0).astype(jnp.float32) + 0.5) * (1.0 / K)
    prof[0] = jnp.exp(jnp.log(height) * (1.0 / 7.0))
    prof[1] = 0.5 * height
    no_level = jnp.zeros((8, 128), jnp.float32)
    for row in range(R):
        W[row, 0:8] = no_level
        W[row, 8 + K:16 + K] = no_level
        F[2, row + 1, 0:8] = no_level
        F[2, row + 1, 8 + K:16 + K] = no_level

    own_ids_copy.wait()

    pl.semaphore_wait(barrier, N - 1 + jnp.where(first, NL - 1, 0))

    class Exchange:
        def __init__(self, send, recv):
            self.send, self.recv, self.items = send, recv, []

        def add(self, tag, src, dst, device, out_if=None, in_if=None):
            i = len(self.items)

            def copy():
                return pltpu.make_async_remote_copy(
                    src_ref=src, dst_ref=dst, send_sem=self.send.at[i], recv_sem=self.recv.at[i],
                    device_id=device, device_id_type=MESH)

            self.items.append((tag, copy, out_if, in_if))
            return self

        def rows(self, tag_up, tag_down, up_src, up_dst, down_src, down_dst):
            self.add(tag_up, up_src, up_dst, {"gx": up_x}, inner_end, inner_start)
            return self.add(tag_down, down_src, down_dst, {"gx": down_x}, inner_start, inner_end)

        def span(self, tag, src, above, below):
            self.add(tag, src, above, {"gy": up_y})
            if sides == 2:
                self.add(tag, src, below, {"gy": down_y})
            return self

        def start(self, *tags):
            for tag, copy, out_if, _ in self.items:
                if tag in tags:
                    if out_if is None:
                        copy().start()
                    else:
                        pl.when(out_if)(lambda: copy().start())

        def wait(self):
            for _, copy, out_if, in_if in self.items:
                if out_if is None:
                    copy().wait()
                else:
                    pl.when(out_if)(lambda: copy().wait_send())
                    pl.when(in_if)(lambda: copy().wait_recv())

    above = sides

    def ids_exchange():
        return Exchange(i_s, i_r).span("s", ID.at[0], ID.at[1], ID.at[above])

    def fields_exchange():
        e = Exchange(a_s, a_r)
        e.rows("r", "r", F.at[:, R, mid], F.at[:, 0, mid], F.at[:, 1, mid], F.at[:, R + 1, mid])
        return e.span("s", EA.at[0], EA.at[1], EA.at[above]).span("s", NM.at[0], NM.at[1], NM.at[above])

    def speed_exchange():
        return Exchange(b_s, b_r).rows("r", "r", U.at[R], U.at[0], U.at[1], U.at[R + 1])

    def source_exchange():
        e = Exchange(c_s, c_r)
        for side, to in ((0, up_y), (1, down_y))[:sides]:
            e.add(blocks - 1, EC.at[blocks - 1], EL.at[side, 0], {"gx": up_x, "gy": to}, inner_end, inner_start)
            e.add(0, EC.at[0], EL.at[side, tiles - 1], {"gx": down_x, "gy": to}, inner_start, inner_end)
        e.rows(
            blocks - 1, 0,
            RR.at[pl.ds(R, H), mid], RR.at[pl.ds(0, H), mid],
            RR.at[pl.ds(H, H), mid], RR.at[pl.ds(H + R, H), mid])
        for b in range(blocks):
            e.span(b, EC.at[b], EL.at[0, b + 1], EL.at[above - 1, b + 1])
        return e.rows(blocks - 1, 0, EC.at[blocks - 1], XE.at[0], EC.at[0], XE.at[1])

    def planes_copy(d):
        return pltpu.make_async_remote_copy(
            src_ref=planes, dst_ref=PL.at[pl.ds(lay * held, held)],
            send_sem=p_s.at[d], recv_sem=p_r.at[d],
            device_id={"layout": lax.rem(lay + d, NL)}, device_id_type=MESH,
        )

    def planes_landing(d):
        source = lax.rem(lay + NL - d, NL)
        return pltpu.make_async_remote_copy(
            src_ref=planes, dst_ref=PL.at[pl.ds(source * held, held)],
            send_sem=p_s.at[d], recv_sem=p_r.at[d],
            device_id={"layout": source}, device_id_type=MESH,
        )

    def first_plane(d, source):
        return pltpu.make_async_remote_copy(
            src_ref=P0.at[lay], dst_ref=P0.at[source],
            send_sem=p_s.at[NL + d], recv_sem=p_r.at[NL + d],
            device_id={"layout": lax.rem(lay + d, NL)}, device_id_type=MESH,
        )

    ids_exchange().start("s")

    @pl.when(first)
    def _():
        held_planes.wait()
        near = jnp.minimum(jnp.maximum(slot[0] - lay * held, 0), held - 1)
        for c in range(4):
            P0[lay, c] = HP[near, c]
        for d in range(1, NL):
            first_plane(d, lay).start()
        for d in range(1, NL):
            planes_copy(d).start()

    lane = lax.broadcasted_iota(jnp.int32, (K, 128), 1)
    level = lax.broadcasted_iota(jnp.int32, (K, 128), 0)
    at_first, at_last = lane == 0, lane == 127
    odd_lane = lax.rem(lane, 2) == 1
    low = K // 2 - RADIUS
    in_band = (level >= low) & (level <= low + 2 * RADIUS)
    lane_8 = lax.broadcasted_iota(jnp.int32, (8, 128), 1)
    level_8 = lax.broadcasted_iota(jnp.int32, (8, 128), 0)
    around_end = lax.rem(lane + 1, 128)
    window = lax.rem(lane + 8, 128)
    place = lax.rem(window, 16)
    group = window // 16
    early = place < 8

    def beside(f, rim):
        return pltpu.roll(jnp.where(at_last, rim, f), 1, 1), pltpu.roll(jnp.where(at_first, rim, f), 127, 1)

    def put(ref, index, f):
        ref[(*index, mid)] = f
        ref[(*index, pl.ds(7, 1))] = f[0:1]
        ref[(*index, pl.ds(8 + K, 1))] = f[K - 1:K]

    def level_pair(ref, index):
        return ref[(*index, pl.ds(7, K))], ref[(*index, pl.ds(9, K))]

    own_ids = ID[0]
    sectors = jnp.zeros((R, 128), jnp.int32)
    runs = sectors
    for t in range(turbines):
        here = own_ids == t
        sectors = jnp.where(here, yaw_sector[0, t], sectors)
        runs = jnp.where(here, active[0, t], runs)
    angle = (sectors.astype(jnp.float32) - 3.5) * YAW_INCREMENT
    FO[2] = jnp.where(own_ids >= 0, jnp.cos(angle), 0.0)
    FO[3] = jnp.where(own_ids >= 0, jnp.sin(angle), 0.0)
    FO[4] = runs.astype(jnp.float32)

    lane_r = lax.broadcasted_iota(jnp.int32, (R, 128), 1)
    shifts = []
    for shift in range(1, 2 * RADIUS + 1):
        shifts.append((1, shift, lane_r >= 128 - shift))
        shifts.append((above, 128 - shift, lane_r < shift))

    def disk_masks():
        names = [ID[0], ID[1], ID[above]]
        for i, (other, amount, wraps) in enumerate(shifts):
            there = names[1] if other == 1 else names[2]
            i_sh = pltpu.roll(jnp.where(wraps, there, names[0]), amount, 1)
            MK[i] = jnp.where(i_sh == names[0], 1.0, 0.0)

    def disk_forces():
        own, before, after = NM[0], NM[1], NM[above]
        total = own
        for i, (other, amount, wraps) in enumerate(shifts):
            n_sh = pltpu.roll(jnp.where(wraps, before if i % 2 == 0 else after, own), amount, 1)
            total = total + jnp.where(MK[i] > 0.5, n_sh, 0.0)
        speed = total / float((2 * RADIUS + 1) ** 2)
        thrust = (-0.5 * THRUST_COEFF * TIME_STEP) * speed * jnp.abs(speed) * FO[4]
        FO[0] = thrust * FO[2]
        FO[1] = thrust * FO[3]

    def disk_sums(row, u, v):
        SU[0, row:row + 1, :] = jnp.sum(jnp.where(in_band, u, 0.0), axis=0, keepdims=True)
        SU[1, row:row + 1, :] = jnp.sum(jnp.where(in_band, v, 0.0), axis=0, keepdims=True)

    def send_span():
        NM[0] = SU[0] * FO[2] + SU[1] * FO[3]
        fields_exchange().start("s")

    width = 128 // groups

    def theta_copy(par, d):
        return pltpu.make_async_remote_copy(
            src_ref=TS.at[par, 0], dst_ref=TS.at[par, d],
            send_sem=t_s.at[par, d], recv_sem=t_r.at[par, d],
            device_id=device_of(lax.rem(s + d, N)), device_id_type=MESH,
        )

    def send_theta(par, total):
        packed = jnp.zeros((8, 128), jnp.float32)
        for g in range(groups):
            part = jnp.sum(total[g * 8:(g + 1) * 8], axis=1, keepdims=True)
            packed = jnp.where(lane_8 // width == g, part, packed)
        TS[par, 0] = packed
        for d in range(1, N):
            theta_copy(par, d).start()

    def mean_theta(par):
        for d in range(1, N):
            theta_copy(par, d).wait()
        total = TS[par, 0]
        for d in range(1, N):
            total = total + TS[par, d]
        total = total * (TIME_STEP * BUOYANCY / columns)
        for g in range(groups):
            MB[8 * g:8 * g + 8] = jnp.broadcast_to(total[:, g * width:g * width + 1], (8, 128))

    def gather(items, place_of, width):
        while len(items) > 1:
            merged = []
            for a, b in zip(items[::2], items[1::2]):
                if a is None and b is None:
                    merged.append(None)
                    continue
                moved = zero if b is None else pltpu.roll(b, width, 1)
                merged.append(jnp.where(place_of < width, zero if a is None else a, moved))
            items, width = merged, 2 * width
        return items[0]

    def unpack16(packed, j):
        return pltpu.roll(packed, 128 - 16 * j, 1) if j else packed

    own_theta.wait()
    total = zero
    for row in range(R):
        warm = T[row + 1, mid] + prof[1]
        put(T, (row + 1,), warm)
        if row in (0, R - 1):
            F[3, row + 1, mid] = warm
        total = total + warm
    send_theta(0, total)
    own_state.wait()
    rims = []
    for row in range(R):
        u = F[0, row + 1, mid] + prof[0]
        v = F[1, row + 1, mid]
        put(F, (0, row + 1), u)
        put(F, (1, row + 1), v)
        disk_sums(row, u, v)
        rims.append(gather([u, v, F[2, row + 1, mid], T[row + 1, mid]], around_end, 2))
    EA[0] = gather(rims, around_end, 8)
    fields_exchange().start("r")
    send_span()
    ids_exchange().wait()
    disk_masks()

    def rim_of(row, c):
        return pltpu.roll(EM[...], lax.rem(128 - 8 * row - 2 * c, 128), 1)

    def tendency_row(row):
        x = row + 1
        y_pairs = [beside(F[c, x, mid], rim_of(row, c)) for c in range(3)]
        for g in range(groups):
            k = 8 + 8 * g
            cen, dx, dy, dz, around = [], [], [], [], []
            for c in range(3):
                f = F[c, x, k:k + 8]
                xm, xp = F[c, x - 1, k:k + 8], F[c, x + 1, k:k + 8]
                ym, yp = (f_y[8 * g:8 * g + 8] for f_y in y_pairs[c])
                km, kp = F[c, x, k - 1:k + 7], F[c, x, k + 1:k + 9]
                cen.append(f)
                dx.append(xp - xm)
                dy.append(yp - ym)
                dz.append(kp - km)
                around.append((xp + xm) + (kp + km) + (yp + ym))
            square = 2.0 * (dx[0] * dx[0] + dy[1] * dy[1] + dz[2] * dz[2])
            for shear in (dy[0] + dx[1], dz[0] + dx[2], dz[1] + dy[2]):
                square = square + shear * shear
            nu = (TIME_STEP * VISCOSITY) + (0.5 * TIME_STEP * SMAGORINSKY) * jnp.sqrt(square)
            NU[row, 8 * g:8 * g + 8] = nu
            remain = 1.0 - 6.0 * nu
            half_u, half_v, half_w = ((0.5 * TIME_STEP) * f for f in cen)
            for c in range(3):
                new = (cen[c] * remain + around[c] * nu) - (half_u * dx[c] + half_v * dy[c] + half_w * dz[c])
                if c < 2:
                    if 8 * g <= low + 2 * RADIUS and 8 * g + 7 >= low:
                        at = level_8 + 8 * g
                        band = (at >= low) & (at <= low + 2 * RADIUS)
                        force = FO[c, pl.ds(row, 1), :]
                        new = new + jnp.where(band, jnp.broadcast_to(force, (8, 128)), 0.0)
                else:
                    new = new + ((TIME_STEP * BUOYANCY) * T[x, k:k + 8] - MB[8 * g:8 * g + 8])
                if c == 0:
                    U[x, 8 * g:8 * g + 8] = new
                elif c == 1:
                    V[row, 8 * g:8 * g + 8] = new
                else:
                    W[row, k:k + 8] = new

    def theta_row(row):
        x = row + 1
        y_pair = beside(T[x, mid], rim_of(row, 3))
        parts = []
        for g in range(groups):
            k = 8 + 8 * g
            f = T[x, k:k + 8]
            xm, xp = T[x - 1, k:k + 8], T[x + 1, k:k + 8]
            ym, yp = (f_y[8 * g:8 * g + 8] for f_y in y_pair)
            km, kp = T[x, k - 1:k + 7], T[x, k + 1:k + 9]
            nu = DIFFUSIVITY_RATIO * NU[row, 8 * g:8 * g + 8]
            turn = F[0, x, k:k + 8] * (xp - xm) + F[1, x, k:k + 8] * (yp - ym) + F[2, x, k:k + 8] * (kp - km)
            new = f * (1.0 - 6.0 * nu) + ((xp + xm) + (kp + km) + (yp + ym)) * nu - (0.5 * TIME_STEP) * turn
            TH[row, 8 * g:8 * g + 8] = new
            parts.append(new)
        return parts

    def sources():
        for b in range(blocks):
            rows, rims = [], []
            for j in range(8):
                row = 8 * b + j
                v = V[row]
                v_next = pltpu.roll(v, 1, 1)
                vm = jnp.where(at_first, 0.0, v_next)
                vp = jnp.where(at_last, 0.0, pltpu.roll(v, 127, 1))
                wm, wp = level_pair(W, (row,))
                r = ((U[row + 2] - U[row]) + (vp - vm) + (wp - wm)) * 0.5
                RR[row + H, mid] = r
                rows.append(r)
                rims.append(v_next)
            packed = gather(rows, window, 16)
            OC[b] = packed
            EC[b] = jnp.where(place < 2, pltpu.roll(gather(rims, lane, 16), 120, 1), packed)
            source_exchange().start(b)

    def row_places(t):
        if t == 0:
            return [(i, 8 - H + i) for i in range(H)]
        if t == tiles - 1:
            return [(R + H + i, i) for i in range(H)]
        return [(8 * (t - 1) + j + H, j) for j in range(8)]

    def complete():
        wholes = []
        for t in range(tiles):
            if t in (0, tiles - 1):
                known = dict((j, x) for x, j in row_places(t))
                clean = gather([RR[known[j], mid] if j in known else None for j in range(8)], window, 16)
                own = XE[0 if t == 0 else 1]
            else:
                clean, own = OC[t - 1], EC[t - 1]
            before, after = EL[0, t], EL[above - 1, t]
            left = jnp.where(early, before, clean)
            left = left + 0.5 * jnp.where(place == 7, pltpu.roll(own, 6, 1), 0.0)
            left = left - 0.5 * jnp.where(place == 8, pltpu.roll(before, 8, 1), 0.0)
            right = jnp.where(early, clean, after)
            right = right + 0.5 * jnp.where(place == 7, pltpu.roll(after, 6, 1), 0.0)
            right = right - 0.5 * jnp.where(place == 8, pltpu.roll(own, 8, 1), 0.0)
            put(SR, (0, t), left)
            put(SR, (1, t), right)
            wholes.append(jnp.where(early, right, left))
        for slot_j in range(8):
            for t in range(tiles):
                for x, j in row_places(t):
                    if j == slot_j:
                        put(RR, (x,), jnp.where(at_first | at_last, unpack16(wholes[t], j), RR[x, mid]))

    sixth = jnp.float32(1.0 / 6.0)
    at_start = jnp.where(first, 0.0, sixth).astype(jnp.float32)
    at_end = jnp.where(last, 0.0, sixth).astype(jnp.float32)

    def relax(index, around, centre, source, keep):
        if index == 0:
            return (around * (-1.0 / 6.0) - centre) * keep
        return (around - source) * keep

    def sweep(index, v):
        old = RR if index == 0 else PP[(index - 1) % 2]
        new = PP[index % 2]
        for x in range(H - (v - 1), R + H + (v - 1)):
            keep = at_start if x < H else at_end if x >= R + H else sixth
            for g in range(groups):
                k = 8 + 8 * g
                f = old[x, k:k + 8]
                around = (old[x + 1, k:k + 8] + old[x - 1, k:k + 8])
                around = around + (old[x, k - 1:k + 7] + old[x, k + 1:k + 9])
                around = around + (pltpu.roll(f, 1, 1) + pltpu.roll(f, 127, 1))
                p = relax(index, around, f, RR[x, k:k + 8] if index else None, keep)
                new[x, k:k + 8] = p
                if g == 0:
                    new[x, 7:8] = p[0:1]
                if g == groups - 1:
                    new[x, 8 + K:9 + K] = p[7:8]
        old = SR if index == 0 else SS[(index - 1) % 2]
        new = SS[index % 2]
        for side in range(2):
            for t in range(tiles):
                keep = at_start if t == 0 else at_end if t == tiles - 1 else sixth
                f = old[side, t, mid]
                fm = old[side, t - 1, mid] if t else f
                fp = old[side, t + 1, mid] if t < tiles - 1 else f
                km, kp = level_pair(old, (side, t))
                around = pltpu.roll(jnp.where(group == 7, fm, f), 16, 1)
                around = around + pltpu.roll(jnp.where(group == 0, fp, f), 112, 1)
                around = around + (km + kp) + (pltpu.roll(f, 1, 1) + pltpu.roll(f, 127, 1))
                put(new, (side, t), relax(index, around, f, SR[side, t, mid] if index else None, keep))

    def finish(n):
        p, side = PP[(SWEEPS - 1) % 2], SS[(SWEEPS - 1) % 2]
        edge = (lane < SWEEPS) | (lane >= 128 - SWEEPS)
        wholes, rims = [], []
        for t in range(tiles):
            left, right = side[0, t, mid], side[1, t, mid]
            wholes.append(jnp.where(early, right, left))
            rims.append(jnp.where(early, left, right))

        def merge(x, t, j):
            put(p, (x,), jnp.where(edge, unpack16(wholes[t], j), p[x, mid]))

        merge(H - 1, 0, 7)
        merge(R + H, tiles - 1, 0)
        for j in range(8):
            for b in range(blocks):
                merge(8 * b + j + H, b + 1, j)
                RR[8 * b + j + H, mid] = unpack16(rims[b + 1], j)
        rows = [None] * R
        for row in [0, R - 1] + list(range(1, R - 1)):
            x = row + H
            centre = p[x, mid]
            rim = RR[x, mid]
            ym = pltpu.roll(jnp.where(at_last, rim, centre), 1, 1)
            yp = pltpu.roll(jnp.where(at_first, rim, centre), 127, 1)
            km, kp = level_pair(p, (x,))
            u = U[row + 1] - 0.5 * (p[x + 1, mid] - p[x - 1, mid])
            v = V[row] - 0.5 * (yp - ym)
            w = W[row, mid] - 0.5 * (kp - km)
            warm = TH[row]
            disk_sums(row, u, v)
            put(F, (0, row + 1), u)
            put(F, (1, row + 1), v)
            F[2, row + 1, mid] = w
            put(T, (row + 1,), warm)
            if row in (0, R - 1):
                F[3, row + 1, mid] = warm
            rows[row] = gather([u, v, w, warm], around_end, 2)
            if row == R - 1:
                pl.when(n < STEPS - 1)(lambda: fields_exchange().start("r"))
        EA[0] = gather(rows, around_end, 8)

    def step(n, carry):
        par = lax.rem(n, 2)
        fields_exchange().wait()

        def inflow(held_in, index):
            for c in range(4):
                f = held_in[index, c]
                if c in (0, 3):
                    f = f + prof[0 if c == 0 else 1]
                F[c, 0, mid] = f
                if c == 0:
                    U[0] = f

        @pl.when(first & (n == 0))
        def _():
            for d in range(1, NL):
                first_plane(d, lay).wait_send()
                first_plane(d, lax.rem(lay + NL - d, NL)).wait_recv()
            inflow(P0, lax.div(slot[0], held))

        @pl.when(first & (n == 1))
        def _():
            own_planes.wait()
            for d in range(1, NL):
                planes_copy(d).wait_send()
                planes_landing(d).wait_recv()

        @pl.when(first & (n > 0))
        def _():
            inflow(PL, slot[n])

        @pl.when(last)
        def _():
            for c in range(4):
                F[c, R + 1, mid] = F[c, R, mid]

        T[0, mid] = F[3, 0, mid]
        T[R + 1, mid] = F[3, R + 1, mid]
        EM[...] = jnp.where(odd_lane, EA[1], EA[above])
        disk_forces()
        mean_theta(par)

        def pair(i, c):
            tendency_row(i)
            tendency_row(R - 1 - i)
            pl.when(i == 0)(lambda: speed_exchange().start("r"))
            return c

        lax.fori_loop(0, R // 2, pair, 0)

        @pl.when(last)
        def _():
            U[R + 1] = U[R]

        speed_exchange().wait()
        sources()

        def warm_row(row, parts):
            return tuple(a + b for a, b in zip(parts, theta_row(row)))

        parts = lax.fori_loop(
            0, R // 2, lambda i, c: warm_row(2 * i + 1, warm_row(2 * i, c)), tuple(no_level for _ in range(groups)))

        @pl.when(n < STEPS - 1)
        def _():
            send_theta(1 - par, jnp.concatenate(parts, axis=0))

        source_exchange().wait()
        complete()
        for i in range(SWEEPS):
            sweep(i, H - i)
        finish(n)

        @pl.when(n < STEPS - 1)
        def _():
            send_span()

        return carry

    lax.fori_loop(0, STEPS, step, 0)

    own_out = pltpu.make_async_copy(F.at[pl.ds(0, 3), pl.ds(1, R), mid], out.at[0, pl.ds(0, 3)], loc.at[2])
    theta_out = pltpu.make_async_copy(T.at[pl.ds(1, R), mid], out.at[0, 3], loc.at[4])
    own_out.start()
    theta_out.start()
    own_out.wait()
    theta_out.wait()


def solution(mesh):
    NL, GX, L = mesh.shape["layout"], mesh.shape["gx"], mesh.shape["gy"]

    def local(state, planes, turbine_cell, active, yaw_sector, slot):
        rows, K, cols = state.shape[2:]
        R = rows
        H = SWEEPS + 1
        N = GX * L
        turbines = active.shape[1]
        KP, tiles, sides = K + 16, R // 8 + 2, 1 if L == 2 else 2
        held = planes.shape[0]
        smem = pl.BlockSpec(memory_space=pltpu.SMEM)
        hbm = pl.BlockSpec(memory_space=pltpu.HBM)
        free = pl.BlockSpec(memory_space=pl.ANY)
        f32 = jnp.float32
        dma = pltpu.SemaphoreType.DMA
        return pl.pallas_call(
            functools.partial(
                kernel, NL, GX, L, R, K, H, turbines, held, float(rows * GX * cols * L)
            ),
            out_shape=jax.ShapeDtypeStruct(state.shape, f32),
            in_specs=[smem, smem, smem, hbm, hbm, hbm],
            out_specs=free,
            scratch_shapes=[
                pltpu.VMEM((4, R + 2, KP, cols), f32),
                pltpu.VMEM((R + 2, KP, cols), f32),
                pltpu.VMEM((R, K, cols), f32),
                pltpu.VMEM((R, K, cols), f32),
                pltpu.VMEM((R, K, cols), f32),
                pltpu.VMEM((R, KP, cols), f32),
                pltpu.VMEM((R + 2, K, cols), f32),
                pltpu.VMEM((R + 2 * H, KP, cols), f32),
                pltpu.VMEM((R + 2 * H, KP, cols), f32),
                pltpu.VMEM((R + 2 * H, KP, cols), f32),
                pltpu.VMEM((2, tiles, KP, cols), f32),
                pltpu.VMEM((2, tiles, KP, cols), f32),
                pltpu.VMEM((2, tiles, KP, cols), f32),
                pltpu.VMEM((held * NL, 4, K, cols), f32),
                pltpu.VMEM((sides + 1, R, cols), jnp.int32),
                pltpu.VMEM((2, R, cols), f32),
                pltpu.VMEM((sides + 1, R, cols), f32),
                pltpu.VMEM((5, R, cols), f32),
                pltpu.VMEM((4 * RADIUS, R, cols), f32),
                pltpu.VMEM((2, N, 8, 128), f32),
                pltpu.VMEM((sides + 1, K, cols), f32),
                pltpu.VMEM((K, cols), f32),
                pltpu.VMEM((K, cols), f32),
                pltpu.VMEM((R // 8, K, cols), f32),
                pltpu.VMEM((R // 8, K, cols), f32),
                pltpu.VMEM((sides, tiles, K, cols), f32),
                pltpu.VMEM((2, K, cols), f32),
                pltpu.VMEM((held, 4, K, cols), f32),
                pltpu.VMEM((NL, 4, K, cols), f32),
                pltpu.VMEM((2, K, cols), f32),
                dma((2,)), dma((2,)), dma((2 * NL,)), dma((2 * NL,)),
                dma((6,)), dma((6,)), dma((2,)), dma((2,)),
                dma((4 + sides * tiles,)), dma((4 + sides * tiles,)),
                dma((2, N)), dma((2, N)),
                dma((7,)),
            ],
            compiler_params=pltpu.CompilerParams(
                collective_id=0, has_side_effects=True, vmem_limit_bytes=60 * 1024 * 1024
            ),
        )(slot, active, yaw_sector, turbine_cell, state, planes)

    return jax.shard_map(
        local,
        mesh=mesh,
        in_specs=(
            P("layout", None, "gx", None, "gy"),
            P("layout", None, None, "gy"),
            P("layout", "gx", None, "gy"),
            P("layout", None),
            P("layout", None),
            P(),
        ),
        out_specs=P("layout", None, "gx", None, "gy"),
        check_vma=False,
    )
```
